512 devices in a mesh: obj: 16 (over x, z_hi, core), tile: 32 (over y, z_lo).
Axes of the slice: x: 4, y: 4, z: 16 (z_hi: 2, z_lo: 8; z = z_hi * 8 + z_lo), core: 2. Of those that a mesh axis runs over, the one named last changes fastest.
Arguments:
- checkpoints: bfloat16 [6, 12, 48, 32, 128], P(None, None, 'obj', 'tile'), may hold values from 0.19921875 to 2
- courant: float32 [2, 48, 32, 128], P(None, None, 'tile'), may hold values from -0.6 to 0.6
- insolation: float32 [32, 128], P('tile'), may hold values from 0.3 to 3
- region_mask: int32 [16, 32, 128], P('obj', 'tile'), may hold values 0 or 1
- measure_step: int32 [16], P('obj'), may hold values from 1 to 6
- snr_weight: float32 [12, 48], replicated, may hold values from 0.3 to 3
- diffusion_number: float32 [12, 47], replicated, may hold values from 0.1 to 2
- coupling: float32 [12, 12], replicated, may hold values from -1.75 to 1.75
- recombination: float32 [12], replicated, may hold values from 0.05 to 0.25
Outputs:
- state_adjoint: float32 [16, 12, 48, 32, 128], P('obj', None, None, 'tile')
- driver_grad: float32 [16, 6, 12, 48], P('obj')
The draws below stay inside these ranges and needn't reach their ends.
All inputs are finite; a program needn't handle non-finite values. No bound on the sum of `region_mask` on one device may be relied on, other than what follows from the above.
Results may differ from the reference program's by a relative error of at most 0.0003.
Values may be sent and summed in bfloat16 or wider, within the bound.
A program may use at most 64 MiB of HBM per device.

```python
import math
import jax
import jax.numpy as jnp
from jax import lax

F = 12
L = 48
NLAT = 128
STEPS = 6
NOBJ = 16
NLON = 32
NCELLS = 4096


def with_ends(array, own_key, least, top_value):
    extent = array.shape
    spot = [jax.random.randint(jax.random.fold_in(own_key, axis), (), 0, extent[axis]) for axis in range(len(extent))]
    array = array.at[tuple(spot)].set(least)
    longest = extent.index(max(extent))
    spot[longest] = (spot[longest] + 1) % extent[longest]
    return array.at[tuple(spot)].set(top_value)


def block_scale(rng, shape, split, least, high):
    gain = 1.0
    for axis_at, blocks in split:
        heights = jax.random.uniform(jax.random.fold_in(jax.random.fold_in(rng, 6), axis_at), (blocks,), jnp.float32, least / len(split), high / len(split))
        gain = gain * jnp.repeat(jnp.exp(heights), shape[axis_at] // blocks).reshape((-1,) + (1,) * (len(shape) - 1 - axis_at))
    return gain


def centred(stream_key, dims, deviation, most, kind=jnp.bfloat16):
    result = jax.random.normal(stream_key, dims, jnp.float32) * deviation
    return jnp.minimum(jnp.maximum(result, -most), most).astype(kind)


def setup_inputs(seed: int = 0) -> dict:
    arg_keys = jax.random.split(jax.random.key(seed), 10)
    return {
        "checkpoints": jnp.clip(0.19921875 + 1.8007812 * jax.random.uniform(arg_keys[0], (STEPS, F, L, NLON, NLAT), jnp.float32) ** block_scale(arg_keys[0], (STEPS, F, L, NLON, NLAT), ((2, 16), (3, 32)), -0.2, 0.2), 0.19921875, 2.0).astype(jnp.bfloat16),
        "courant": jnp.clip(jax.random.uniform(arg_keys[1], (2, L, NLON, NLAT), jnp.float32, -0.6, 0.6) * block_scale(arg_keys[1], (2, L, NLON, NLAT), ((2, 32),), -0.4, 0.0), -0.6, 0.6),
        "insolation": jnp.clip(jnp.exp(math.log(3.0) - 2.3025851 * jax.random.uniform(arg_keys[2], (NLON, NLAT), jnp.float32) ** block_scale(arg_keys[2], (NLON, NLAT), ((0, 32),), -0.2, 0.2)), 0.3, 3.0),
        "region_mask": with_ends((jax.random.randint(arg_keys[3], (NOBJ, NLON, NLAT), 0, 2) < 1).astype(jnp.int32), jax.random.fold_in(arg_keys[3], 1), 0, 1),
        "measure_step": with_ends(jax.random.randint(arg_keys[4], (NOBJ,), 1, STEPS + 1), jax.random.fold_in(arg_keys[4], 1), 1, STEPS).astype(jnp.int32),
        "snr_weight": jnp.clip(jnp.exp(jax.random.uniform(arg_keys[5], (F, L), jnp.float32, math.log(0.3), math.log(3.0))), 0.3, 3.0),
        "diffusion_number": jnp.clip(jnp.exp(jax.random.uniform(arg_keys[6], (F, L - 1), jnp.float32, math.log(0.1), math.log(2.0))), 0.1, 2.0),
        "coupling": centred(arg_keys[7], (F, F), F ** -0.5, 1.75, jnp.float32),
        "recombination": jnp.clip(jnp.exp(jax.random.uniform(arg_keys[8], (F,), jnp.float32, math.log(0.05), math.log(0.25))), 0.05, 0.25),
    }


smoothing = 0.2

def advect_back(adjoint, courant):
    eastward = courant[0][None]
    northward = courant[1][None]
    flux = eastward * adjoint
    beside_all = jnp.roll(adjoint, -1, 2) + jnp.roll(adjoint, 1, 2)
    carried = jnp.roll(flux, -1, 2) - jnp.roll(flux, 1, 2)
    lat_pad = jnp.pad(adjoint, ((0, 0), (0, 0), (0, 0), (1, 1)))
    north_flux = jnp.pad(northward * adjoint, ((0, 0), (0, 0), (0, 0), (1, 1)))
    beside_all = beside_all + lat_pad[..., 2:] + lat_pad[..., :-2]
    carried = carried + north_flux[..., 2:] - north_flux[..., :-2]
    return (1.0 - 4.0 * smoothing) * adjoint + smoothing * beside_all + 0.5 * carried

def reference(checkpoints, courant, insolation, region_mask, measure_step, snr_weight, diffusion_number, coupling, recombination):
    below = jnp.pad(diffusion_number, ((0, 0), (1, 0)))
    above = jnp.pad(diffusion_number, ((0, 0), (0, 1)))
    middle = 1.0 + below + above

    def one_objective(index):
        impulse = region_mask[index].astype(jnp.float32)[None, None] * snr_weight[:, :, None, None]
        adjoint = jnp.zeros((F, L, NLON, NLAT), jnp.float32)
        grads = [None] * STEPS
        for back in range(STEPS):
            moment = STEPS - 1 - back
            arrive = (measure_step[index] == moment + 1).astype(jnp.float32)
            adjoint = adjoint + arrive * impulse
            advected = advect_back(adjoint, courant)
            solved = lax.linalg.tridiagonal_solve(-below, middle, -above, advected.reshape(F, L, NLON * NLAT)).reshape(F, L, NLON, NLAT)
            grads[moment] = jnp.einsum('flxy,xy->fl', solved, insolation, precision=lax.Precision.HIGHEST) / NCELLS
            state = checkpoints[moment].astype(jnp.float32)
            mixing = jnp.einsum('fg,flxy->glxy', coupling, solved, precision=lax.Precision.HIGHEST)
            adjoint = solved + mixing - 2.0 * recombination[:, None, None, None] * state * solved
        return (adjoint, jnp.stack(grads))
    adjoints, gradients = lax.map(one_objective, jnp.arange(NOBJ, dtype=jnp.int32))
    return (adjoints, gradients)
```

```python
import functools

import jax
import jax.numpy as jnp
from jax import lax
from jax.experimental import pallas as pl
from jax.experimental.pallas import tpu as pltpu
from jax.sharding import PartitionSpec as P

smoothing = 0.2
MESH = pl.DeviceIdType.MESH
F = 12
L = 48
ROWS = F * L
NZ = 8
LAT = 16
TILES = 9
SLAB = 72
STEPS = 6


def kernel(
    ny, cp_ref, wind_ref, insol_ref, imp_ref, snr_ref, kb_ref, coup_ref, rec_ref,
    out_ref, grad_ref,
    adj, adv, sol, coef, inv, mats, fwd, piv, edge_out, edge_in, swap_out, swap_in,
    send_sem, recv_sem, swap_send, swap_recv,
):
    obj = lax.axis_index("obj")
    tile = lax.axis_index("tile")
    y = tile // NZ
    z = lax.rem(tile, NZ)
    east = lax.rem(y + 1, ny) * NZ + z
    west = lax.rem(y + ny - 1, ny) * NZ + z

    edge_in[...] = jnp.zeros_like(edge_in)
    barrier = pltpu.get_barrier_semaphore()
    for peer in (east, west):
        pl.semaphore_signal(barrier, inc=1, device_id=(obj, peer), device_id_type=MESH)
    for hop in range(1, NZ):
        peer = y * NZ + lax.rem(z + hop, NZ)
        pl.semaphore_signal(barrier, inc=1, device_id=(obj, peer), device_id_type=MESH)

    lane = lax.broadcasted_iota(jnp.int32, (8, 128), 1)
    block = lane // LAT
    inside = lax.rem(lane, LAT)

    for half in range(2):
        rows = pl.ds(half * L, L)
        coef[0, rows] = smoothing + 0.5 * wind_ref[0]
        coef[1, rows] = smoothing - 0.5 * wind_ref[0]
        coef[2, rows] = smoothing + 0.5 * wind_ref[1]
        coef[3, rows] = smoothing - 0.5 * wind_ref[1]

    unit = lax.broadcasted_iota(jnp.int32, (16, 128), 1)
    first = 1.0 / (1.0 + kb_ref[0])
    piv[0] = first
    fwd[0] = (unit == 0).astype(jnp.float32)

    def down(l, before):
        inverse, value = before
        below = kb_ref[l - 1]
        weight = below * inverse
        inverse = 1.0 / (1.0 + below + kb_ref[l] - below * weight)
        value = jnp.where(unit == l, 1.0, 0.0) + weight * value
        piv[l] = inverse
        fwd[l] = value
        return inverse, value

    last = lax.fori_loop(1, L, down, (first, (unit == 0).astype(jnp.float32)))
    bottom = last[1] * last[0]
    inv[pl.ds((L - 1) * 16, 16)] = bottom

    def up(i, after):
        l = L - 2 - i
        value = (fwd[l] + kb_ref[l] * after) * piv[l]
        inv[pl.ds(pl.multiple_of(l * 16, 16), 16)] = value
        return value

    lax.fori_loop(0, L - 1, up, bottom)
    for f in range(F):
        matrix = inv[pl.ds(f, L, stride=16), :]
        high = matrix.astype(jnp.bfloat16)
        mats[f, pl.ds(0, L)] = high
        mats[f, pl.ds(L, L)] = (matrix - high.astype(jnp.float32)).astype(jnp.bfloat16)

    adj[...] = jnp.zeros_like(adj)
    grad_ref[...] = jnp.zeros_like(grad_ref)
    pl.semaphore_wait(barrier, NZ + 1)

    def at(k, j):
        return pl.ds(pl.multiple_of(SLAB * k + 8 * j, 8), 8)

    def share(way, k, j):
        return coef[way, pl.ds(pl.multiple_of((SLAB * k) % L + 8 * j, 8), 8), :]

    def edge_copy(t, way, peer):
        return pltpu.make_async_remote_copy(
            src_ref=edge_out.at[t, way],
            dst_ref=edge_in.at[t, way],
            send_sem=send_sem.at[t, way],
            recv_sem=recv_sem.at[t, way],
            device_id=(obj, peer),
            device_id_type=MESH,
        )

    def step(t, carry):
        s = STEPS - 1 - t
        impulse = jnp.broadcast_to(imp_ref[pl.ds(s, 1), :], (8, 128))

        def pack(j, c):
            held = [jnp.zeros((8, 128), jnp.float32)] * 4
            for k in range(8):
                a = adj[at(k, j), :] + snr_ref[at(k, j), :] * impulse
                adj[at(k, j), :] = a
                shifts = (16 * k, 16 * (k + 1), k, k - 15)
                for way in range(4):
                    moved = share(way, k, j) * a
                    turn = shifts[way] % 128
                    if turn:
                        moved = pltpu.roll(moved, turn, 1)
                    spot = block == k if way < 2 else inside == k
                    held[way] = jnp.where(spot, moved, held[way])
            for way in range(4):
                edge_out[t, way, pl.ds(pl.multiple_of(8 * j, 8), 8), :] = held[way]
            return c

        lax.fori_loop(0, TILES, pack, 0)
        edge_copy(t, 0, west).start()
        edge_copy(t, 1, east).start()

        @pl.when(z > 0)
        def _():
            edge_copy(t, 2, tile - 1).start()

        @pl.when(z < NZ - 1)
        def _():
            edge_copy(t, 3, tile + 1).start()

        def interior(j, c):
            for k in range(8):
                a = adj[at(k, j), :]
                to_west = pltpu.roll(share(0, k, j) * a, 128 - LAT, 1)
                to_east = pltpu.roll(share(1, k, j) * a, LAT, 1)
                to_south = pltpu.roll(share(2, k, j) * a, 127, 1)
                to_north = pltpu.roll(share(3, k, j) * a, 1, 1)
                adv[at(k, j), :] = (
                    (1.0 - 4.0 * smoothing) * a
                    + jnp.where(block < 7, to_west, 0.0)
                    + jnp.where(block > 0, to_east, 0.0)
                    + jnp.where(inside < LAT - 1, to_south, 0.0)
                    + jnp.where(inside > 0, to_north, 0.0)
                )
            return c

        lax.fori_loop(0, TILES, interior, 0)
        edge_copy(t, 0, west).wait()
        edge_copy(t, 1, east).wait()

        @pl.when(z > 0)
        def _():
            edge_copy(t, 2, tile - 1).wait_send()
            edge_copy(t, 3, tile - 1).wait_recv()

        @pl.when(z < NZ - 1)
        def _():
            edge_copy(t, 3, tile + 1).wait_send()
            edge_copy(t, 2, tile + 1).wait_recv()

        def turned(value, amount):
            return pltpu.roll(value, amount % 128, 1) if amount % 128 else value

        def unpack(j, c):
            got = [edge_in[t, way, pl.ds(pl.multiple_of(8 * j, 8), 8), :] for way in range(4)]
            for k in range(8):
                along = jnp.where(
                    block == 7,
                    turned(got[0], 112 - 16 * k),
                    jnp.where(block == 0, turned(got[1], -16 * k), 0.0),
                )
                across = jnp.where(
                    inside == LAT - 1,
                    turned(got[2], 15 - k),
                    jnp.where(inside == 0, turned(got[3], -k), 0.0),
                )
                adv[at(k, j), :] = adv[at(k, j), :] + along + across
            return c

        lax.fori_loop(0, TILES, unpack, 0)

        insol = insol_ref[pl.ds(0, 1), :]
        wide = lax.broadcasted_iota(jnp.int32, (L, 128), 1)
        for f in range(F):
            rows = pl.ds(f * L, L)
            x = adv[rows, :]
            high = x.astype(jnp.bfloat16)
            low = (x - high.astype(jnp.float32)).astype(jnp.bfloat16)
            both = jnp.dot(
                mats[f][:, :L],
                jnp.concatenate([high, low], axis=1),
                preferred_element_type=jnp.float32,
            )
            solved = both[:L, :128] + (both[:L, 128:] + both[L:, :128])
            sol[rows, :] = solved
            total = jnp.sum(solved * insol, axis=1, keepdims=True)
            grad_ref[rows, :] = jnp.where(wide == s, total, grad_ref[rows, :])

        def mix(i, c):
            def spot(g):
                return pl.ds(pl.multiple_of(g * L + 16 * i, 16), 16)

            parts = [sol[spot(f), :] for f in range(F)]
            for g in range(F):
                state = cp_ref[s, g, pl.ds(pl.multiple_of(16 * i, 16), 16), :]
                total = parts[g] - (2.0 * rec_ref[0, g]) * (state.astype(jnp.float32) * parts[g])
                for f in range(F):
                    total = total + coup_ref[f, g] * parts[f]
                adj[spot(g), :] = total
            return c

        lax.fori_loop(0, L // 16, mix, 0)
        return carry

    lax.fori_loop(0, STEPS, step, 0)

    def spread(j, c):
        turned = [
            pltpu.roll(adj[at(k, j), :], 16 * k, 1) if k else adj[at(k, j), :] for k in range(8)
        ]
        for d in range(NZ):
            piece = turned[0]
            for k in range(1, 8):
                piece = jnp.where(block == (d + k) % 8, turned[k], piece)
            swap_out[d, pl.ds(pl.multiple_of(8 * j, 8), 8), :] = piece
        return c

    lax.fori_loop(0, TILES, spread, 0)

    def swap_copy(hop):
        target = lax.rem(z + hop, NZ)
        return pltpu.make_async_remote_copy(
            src_ref=swap_out.at[target],
            dst_ref=swap_in.at[hop],
            send_sem=swap_send.at[hop],
            recv_sem=swap_recv.at[hop],
            device_id=(obj, y * NZ + target),
            device_id_type=MESH,
        )

    for hop in range(1, NZ):
        swap_copy(hop).start()
    swap_in[0] = swap_out[z]
    for hop in range(1, NZ):
        swap_copy(hop).wait()

    def collect(j, c):
        got = [
            pltpu.roll(
                swap_in[hop, pl.ds(pl.multiple_of(8 * j, 8), 8), :],
                lax.rem(128 + 128 - 16 * (z + hop), 128),
                1,
            )
            for hop in range(NZ)
        ]
        for k in range(8):
            held = got[0]
            for hop in range(1, NZ):
                held = jnp.where(block == (k - hop) % 8, got[hop], held)
            out_ref[at(k, j), :] = pltpu.roll(held, lax.rem(16 * z + 128 - 16 * k, 128), 1)
        return c

    lax.fori_loop(0, TILES, collect, 0)


def per_device(
    checkpoints,
    courant,
    insolation,
    region_mask,
    measure_step,
    snr_weight,
    diffusion_number,
    coupling,
    recombination,
):
    tiles = lax.axis_size("tile")
    ny = tiles // NZ
    chunk = checkpoints.shape[2]
    groups = [[row * NZ + z for z in range(NZ)] for row in range(ny)]
    rows = jnp.concatenate(
        [
            checkpoints.reshape(STEPS * F * chunk, 128).astype(jnp.float32),
            courant.reshape(2 * L, 128),
            insolation,
            region_mask[0].astype(jnp.float32),
        ]
    )
    count = rows.shape[0]
    rows = rows.reshape(count, NZ, LAT).transpose(1, 0, 2)
    rows = lax.all_to_all(rows, "tile", 0, 0, axis_index_groups=groups, tiled=True)
    rows = rows.transpose(1, 0, 2).reshape(count, 128)
    own = STEPS * F * chunk
    state = rows[:own].reshape(STEPS, F, chunk, 128).astype(jnp.bfloat16)
    state = lax.all_gather(state, "obj", axis=2, tiled=True)
    wind = rows[own : own + 2 * L].reshape(2, L, 128)
    insol = rows[own + 2 * L :][:1]
    mask = rows[own + 2 * L + 1 :][:1]
    moments = jnp.arange(1, 9, dtype=jnp.int32)
    impulses = (measure_step[0] == moments).astype(jnp.float32)[:, None] * mask
    weights = jnp.broadcast_to(snr_weight.reshape(ROWS, 1), (ROWS, 128))
    rates = jnp.pad(diffusion_number.T, ((0, 1), (0, 4)))
    rates = jnp.broadcast_to(rates[:, :, None], (L, 16, 128))

    vmem = pl.BlockSpec(memory_space=pltpu.VMEM)
    smem = pl.BlockSpec(memory_space=pltpu.SMEM)
    f32 = jnp.float32
    out, sums = pl.pallas_call(
        functools.partial(kernel, ny),
        out_shape=(
            jax.ShapeDtypeStruct((ROWS, 128), f32),
            jax.ShapeDtypeStruct((ROWS, 128), f32),
        ),
        in_specs=[vmem] * 6 + [smem] * 2,
        out_specs=(vmem, vmem),
        scratch_shapes=[
            pltpu.VMEM((ROWS, 128), f32),
            pltpu.VMEM((ROWS, 128), f32),
            pltpu.VMEM((ROWS, 128), f32),
            pltpu.VMEM((4, 2 * L, 128), f32),
            pltpu.VMEM((L * 16, 128), f32),
            pltpu.VMEM((F, 2 * L, 128), jnp.bfloat16),
            pltpu.VMEM((L, 16, 128), f32),
            pltpu.VMEM((L, 16, 128), f32),
            pltpu.VMEM((STEPS, 4, SLAB, 128), f32),
            pltpu.VMEM((STEPS, 4, SLAB, 128), f32),
            pltpu.VMEM((NZ, SLAB, 128), f32),
            pltpu.VMEM((NZ, SLAB, 128), f32),
            pltpu.SemaphoreType.DMA((STEPS, 4)),
            pltpu.SemaphoreType.DMA((STEPS, 4)),
            pltpu.SemaphoreType.DMA((NZ,)),
            pltpu.SemaphoreType.DMA((NZ,)),
        ],
        compiler_params=pltpu.CompilerParams(collective_id=0, has_side_effects=True),
    )(
        state,
        wind,
        jnp.broadcast_to(insol, (8, 128)),
        impulses,
        weights,
        rates,
        coupling,
        recombination[None],
    )
    sums = lax.psum(sums[:, :STEPS].T, "tile") / (tiles * 128)
    return out.reshape(1, F, L, 1, 128), sums.reshape(1, STEPS, F, L)


def solution(mesh):
    return jax.shard_map(
        per_device,
        mesh=mesh,
        in_specs=(
            P(None, None, "obj", "tile", None),
            P(None, None, "tile", None),
            P("tile", None),
            P("obj", "tile", None),
            P("obj"),
            P(),
            P(),
            P(),
            P(),
        ),
        out_specs=(P("obj", None, None, "tile", None), P("obj", None, None, None)),
        check_vma=False,
    )
```

```python
import functools

import jax
import jax.numpy as jnp
from jax import lax
from jax.experimental import pallas as pl
from jax.experimental.pallas import tpu as pltpu
from jax.sharding import PartitionSpec as P

smoothing = 0.2
MESH = pl.DeviceIdType.MESH
F = 12
L = 48
ROWS = F * L
NZ = 8
LAT = 16
TILES = 9
SLAB = 72
STEPS = 6


def kernel(
    ny, cp_ref, wind_ref, insol_ref, imp_ref, snr_ref, kb_ref, coup_ref, rec_ref,
    out_ref, grad_ref,
    adj, adv, sol, coef, inv, mats, fwd, piv, edge_out, edge_in, swap_out, swap_in,
    gathered, loose, state, sum_out, sum_y, part_out, sum_z,
    send_sem, recv_sem, swap_send, swap_recv, gather_send, gather_recv,
    y_send, y_recv, z_send, z_recv,
):
    obj = lax.axis_index("obj")
    tile = lax.axis_index("tile")
    y = tile // NZ
    z = lax.rem(tile, NZ)
    east = lax.rem(y + 1, ny) * NZ + z
    west = lax.rem(y + ny - 1, ny) * NZ + z
    x = obj // 4
    far = lax.rem(obj // 2, 2)
    core = lax.rem(obj, 2)

    def chunk(at_x, at_far, at_core):
        return at_x * 4 + at_far * 2 + at_core

    partner = chunk(x, 1 - far, core)
    other = chunk(x, far, 1 - core)
    beside = [chunk(lax.rem(x + h, 4), far, core) for h in range(1, 4)]

    edge_in[...] = jnp.zeros_like(edge_in)
    barrier = pltpu.get_barrier_semaphore()
    for peer in [partner, other] + beside:
        pl.semaphore_signal(barrier, inc=1, device_id=(peer, tile), device_id_type=MESH)
    for hop in range(1, ny):
        peer = lax.rem(y + hop, ny) * NZ + z
        pl.semaphore_signal(barrier, inc=1, device_id=(obj, peer), device_id_type=MESH)
    for hop in range(1, NZ):
        peer = y * NZ + lax.rem(z + hop, NZ)
        pl.semaphore_signal(barrier, inc=1, device_id=(obj, peer), device_id_type=MESH)

    lane = lax.broadcasted_iota(jnp.int32, (8, 128), 1)
    block = lane // LAT
    inside = lax.rem(lane, LAT)

    for half in range(2):
        rows = pl.ds(half * L, L)
        coef[0, rows] = smoothing + 0.5 * wind_ref[0]
        coef[1, rows] = smoothing - 0.5 * wind_ref[0]
        coef[2, rows] = smoothing + 0.5 * wind_ref[1]
        coef[3, rows] = smoothing - 0.5 * wind_ref[1]

    unit = lax.broadcasted_iota(jnp.int32, (16, 128), 1)
    first = 1.0 / (1.0 + kb_ref[0])
    piv[0] = first
    fwd[0] = (unit == 0).astype(jnp.float32)

    def down(l, before):
        inverse, value = before
        below = kb_ref[l - 1]
        weight = below * inverse
        inverse = 1.0 / (1.0 + below + kb_ref[l] - below * weight)
        value = jnp.where(unit == l, 1.0, 0.0) + weight * value
        piv[l] = inverse
        fwd[l] = value
        return inverse, value

    last = lax.fori_loop(1, L, down, (first, (unit == 0).astype(jnp.float32)))
    bottom = last[1] * last[0]
    inv[pl.ds((L - 1) * 16, 16)] = bottom

    def up(i, after):
        l = L - 2 - i
        value = (fwd[l] + kb_ref[l] * after) * piv[l]
        inv[pl.ds(pl.multiple_of(l * 16, 16), 16)] = value
        return value

    lax.fori_loop(0, L - 1, up, bottom)
    for f in range(F):
        matrix = inv[pl.ds(f, L, stride=16), :]
        high = matrix.astype(jnp.bfloat16)
        mats[f, pl.ds(0, L)] = high
        mats[f, pl.ds(L, L)] = (matrix - high.astype(jnp.float32)).astype(jnp.bfloat16)

    adj[...] = jnp.zeros_like(adj)
    gathered[obj] = cp_ref[...]
    pl.semaphore_wait(barrier, 5 + ny - 1 + NZ - 1)

    def gather_copy(s, n, slot, peer, source=None):
        return pltpu.make_async_remote_copy(
            src_ref=gathered.at[slot, s] if source is None else source,
            dst_ref=gathered.at[slot, s],
            send_sem=gather_send.at[s, n],
            recv_sem=gather_recv.at[s, slot],
            device_id=(peer, tile),
            device_id_type=MESH,
        )

    def near_slots():
        return [chunk(lax.rem(x + h, 4), w, core) for h in range(1, 4) for w in range(2)]

    def gather_own(s):
        for n, peer in enumerate([partner] + beside + [other]):
            gather_copy(s, n, obj, peer, cp_ref.at[s]).start()

    def gather_far(s):
        gather_copy(s, 0, partner, partner).wait_recv()
        for n, peer in enumerate(beside + [other]):
            gather_copy(s, 5 + n, partner, peer).start()

    def gather_near(s):
        for n, slot in enumerate(near_slots()):
            gather_copy(s, 9 + n, slot, other).wait_recv()
            gather_copy(s, 9 + n, slot, other).start()

    def gather_end(s):
        for at_x in range(4):
            for w in range(2):
                gather_copy(s, 0, chunk(at_x, w, 1 - core), other).wait_recv()
        for slot in range(16):
            loose[pl.ds(40 * slot, 36), :] = gathered[slot, s].astype(jnp.float32)
        for f in range(F):
            for i in range(3):
                state[pl.ds(f * L + i, 16, stride=3), :] = loose[
                    pl.ds(3 * f + i, 16, stride=40), :
                ]

    def send_own(t, c):
        gather_own(STEPS - 1 - t)
        return c

    lax.fori_loop(0, STEPS, send_own, 0)

    def y_copy(s, hop):
        return pltpu.make_async_remote_copy(
            src_ref=sum_out.at[s],
            dst_ref=sum_y.at[s, hop - 1],
            send_sem=y_send.at[s, hop - 1],
            recv_sem=y_recv.at[s, hop - 1],
            device_id=(obj, lax.rem(y + hop, ny) * NZ + z),
            device_id_type=MESH,
        )

    def z_copy(s, hop):
        return pltpu.make_async_remote_copy(
            src_ref=part_out.at[s],
            dst_ref=sum_z.at[s, hop - 1],
            send_sem=z_send.at[s, hop - 1],
            recv_sem=z_recv.at[s, hop - 1],
            device_id=(obj, y * NZ + lax.rem(z + hop, NZ)),
            device_id_type=MESH,
        )

    def sums_on(s):
        total = sum_out[s]
        for hop in range(1, ny):
            y_copy(s, hop).wait()
            total = total + sum_y[s, hop - 1]
        part_out[s] = total
        for hop in range(1, NZ):
            z_copy(s, hop).start()

    def at(k, j):
        return pl.ds(pl.multiple_of(SLAB * k + 8 * j, 8), 8)

    def share(way, k, j):
        return coef[way, pl.ds(pl.multiple_of((SLAB * k) % L + 8 * j, 8), 8), :]

    def edge_copy(t, way, peer):
        return pltpu.make_async_remote_copy(
            src_ref=edge_out.at[t, way],
            dst_ref=edge_in.at[t, way],
            send_sem=send_sem.at[t, way],
            recv_sem=recv_sem.at[t, way],
            device_id=(obj, peer),
            device_id_type=MESH,
        )

    gather_far(STEPS - 1)
    gather_near(STEPS - 1)
    gather_far(STEPS - 2)

    def step(t, carry):
        s = STEPS - 1 - t
        impulse = jnp.broadcast_to(imp_ref[pl.ds(s, 1), :], (8, 128))

        def pack(j, c):
            held = [jnp.zeros((8, 128), jnp.float32)] * 4
            for k in range(8):
                a = adj[at(k, j), :] + snr_ref[at(k, j), :] * impulse
                adj[at(k, j), :] = a
                shifts = (16 * k, 16 * (k + 1), k, k - 15)
                for way in range(4):
                    moved = share(way, k, j) * a
                    turn = shifts[way] % 128
                    if turn:
                        moved = pltpu.roll(moved, turn, 1)
                    spot = block == k if way < 2 else inside == k
                    held[way] = jnp.where(spot, moved, held[way])
            for way in range(4):
                edge_out[t, way, pl.ds(pl.multiple_of(8 * j, 8), 8), :] = held[way]
            return c

        lax.fori_loop(0, TILES, pack, 0)
        edge_copy(t, 0, west).start()
        edge_copy(t, 1, east).start()

        @pl.when(z > 0)
        def _():
            edge_copy(t, 2, tile - 1).start()

        @pl.when(z < NZ - 1)
        def _():
            edge_copy(t, 3, tile + 1).start()

        def interior(j, c):
            for k in range(8):
                a = adj[at(k, j), :]
                to_west = pltpu.roll(share(0, k, j) * a, 128 - LAT, 1)
                to_east = pltpu.roll(share(1, k, j) * a, LAT, 1)
                to_south = pltpu.roll(share(2, k, j) * a, 127, 1)
                to_north = pltpu.roll(share(3, k, j) * a, 1, 1)
                adv[at(k, j), :] = (
                    (1.0 - 4.0 * smoothing) * a
                    + jnp.where(block < 7, to_west, 0.0)
                    + jnp.where(block > 0, to_east, 0.0)
                    + jnp.where(inside < LAT - 1, to_south, 0.0)
                    + jnp.where(inside > 0, to_north, 0.0)
                )
            return c

        lax.fori_loop(0, TILES, interior, 0)

        @pl.when(t < STEPS - 1)
        def _():
            gather_near(s - 1)

        @pl.when(t < STEPS - 2)
        def _():
            gather_far(s - 2)

        edge_copy(t, 0, west).wait()
        edge_copy(t, 1, east).wait()

        @pl.when(z > 0)
        def _():
            edge_copy(t, 2, tile - 1).wait_send()
            edge_copy(t, 3, tile - 1).wait_recv()

        @pl.when(z < NZ - 1)
        def _():
            edge_copy(t, 3, tile + 1).wait_send()
            edge_copy(t, 2, tile + 1).wait_recv()

        def turned(value, amount):
            return pltpu.roll(value, amount % 128, 1) if amount % 128 else value

        def unpack(j, c):
            got = [edge_in[t, way, pl.ds(pl.multiple_of(8 * j, 8), 8), :] for way in range(4)]
            for k in range(8):
                along = jnp.where(
                    block == 7,
                    turned(got[0], 112 - 16 * k),
                    jnp.where(block == 0, turned(got[1], -16 * k), 0.0),
                )
                across = jnp.where(
                    inside == LAT - 1,
                    turned(got[2], 15 - k),
                    jnp.where(inside == 0, turned(got[3], -k), 0.0),
                )
                adv[at(k, j), :] = adv[at(k, j), :] + along + across
            return c

        lax.fori_loop(0, TILES, unpack, 0)

        @pl.when(t > 0)
        def _():
            sums_on(s + 1)

        insol = insol_ref[pl.ds(0, 1), :]
        sums = jnp.zeros((8, 128), jnp.float32)
        for f in range(F):
            rows = pl.ds(f * L, L)
            x = adv[rows, :]
            high = x.astype(jnp.bfloat16)
            low = (x - high.astype(jnp.float32)).astype(jnp.bfloat16)
            both = jnp.dot(
                mats[f][:, :L],
                jnp.concatenate([high, low], axis=1),
                preferred_element_type=jnp.float32,
            )
            solved = both[:L, :128] + (both[:L, 128:] + both[L:, :128])
            sol[rows, :] = solved
            total = jnp.sum(solved * insol, axis=1, keepdims=True)
            for q in range(L // 8):
                sums = jnp.where(lane == f * (L // 8) + q, total[8 * q : 8 * q + 8], sums)
        sum_out[s] = sums
        for hop in range(1, ny):
            y_copy(s, hop).start()
        gather_end(s)

        def mix(i, c):
            def spot(g):
                return pl.ds(pl.multiple_of(g * L + 16 * i, 16), 16)

            parts = [sol[spot(f), :] for f in range(F)]
            for g in range(F):
                total = parts[g] - (2.0 * rec_ref[0, g]) * (state[spot(g), :] * parts[g])
                for f in range(F):
                    total = total + coup_ref[f, g] * parts[f]
                adj[spot(g), :] = total
            return c

        lax.fori_loop(0, L // 16, mix, 0)
        return carry

    lax.fori_loop(0, STEPS, step, 0)

    def spread(j, c):
        turned = [
            pltpu.roll(adj[at(k, j), :], 16 * k, 1) if k else adj[at(k, j), :] for k in range(8)
        ]
        for d in range(NZ):
            piece = turned[0]
            for k in range(1, 8):
                piece = jnp.where(block == (d + k) % 8, turned[k], piece)
            swap_out[d, pl.ds(pl.multiple_of(8 * j, 8), 8), :] = piece
        return c

    lax.fori_loop(0, TILES, spread, 0)

    def swap_copy(hop):
        target = lax.rem(z + hop, NZ)
        return pltpu.make_async_remote_copy(
            src_ref=swap_out.at[target],
            dst_ref=swap_in.at[hop],
            send_sem=swap_send.at[hop],
            recv_sem=swap_recv.at[hop],
            device_id=(obj, y * NZ + target),
            device_id_type=MESH,
        )

    for hop in range(1, NZ):
        swap_copy(hop).start()
    swap_in[0] = swap_out[z]
    sums_on(0)
    for hop in range(1, NZ):
        swap_copy(hop).wait()

    def collect(j, c):
        got = [
            pltpu.roll(
                swap_in[hop, pl.ds(pl.multiple_of(8 * j, 8), 8), :],
                lax.rem(128 + 128 - 16 * (z + hop), 128),
                1,
            )
            for hop in range(NZ)
        ]
        for k in range(8):
            held = got[0]
            for hop in range(1, NZ):
                held = jnp.where(block == (k - hop) % 8, got[hop], held)
            out_ref[at(k, j), :] = pltpu.roll(held, lax.rem(16 * z + 128 - 16 * k, 128), 1)
        return c

    lax.fori_loop(0, TILES, collect, 0)

    def finish(s, c):
        total = part_out[s]
        for hop in range(1, NZ):
            z_copy(s, hop).wait()
            total = total + sum_z[s, hop - 1]
        grad_ref[s] = total
        for n in range(15):
            gather_copy(s, n, obj, other).wait_send()
        return c

    lax.fori_loop(0, STEPS, finish, 0)


def per_device(
    checkpoints,
    courant,
    insolation,
    region_mask,
    measure_step,
    snr_weight,
    diffusion_number,
    coupling,
    recombination,
):
    tiles = lax.axis_size("tile")
    ny = tiles // NZ
    chunk = checkpoints.shape[2]
    groups = [[row * NZ + z for z in range(NZ)] for row in range(ny)]
    rows = jnp.concatenate(
        [
            checkpoints.reshape(STEPS * F * chunk, 128).astype(jnp.float32),
            courant.reshape(2 * L, 128),
            insolation,
            region_mask[0].astype(jnp.float32),
        ]
    )
    count = rows.shape[0]
    rows = rows.reshape(count, NZ, LAT).transpose(1, 0, 2)
    rows = lax.all_to_all(rows, "tile", 0, 0, axis_index_groups=groups, tiled=True)
    rows = rows.transpose(1, 0, 2).reshape(count, 128)
    own = STEPS * F * chunk
    state = rows[:own].reshape(STEPS, F * chunk, 128).astype(jnp.bfloat16)
    wind = rows[own : own + 2 * L].reshape(2, L, 128)
    insol = rows[own + 2 * L :][:1]
    mask = rows[own + 2 * L + 1 :][:1]
    moments = jnp.arange(1, 9, dtype=jnp.int32)
    impulses = (measure_step[0] == moments).astype(jnp.float32)[:, None] * mask
    weights = jnp.broadcast_to(snr_weight.reshape(ROWS, 1), (ROWS, 128))
    rates = jnp.pad(diffusion_number.T, ((0, 1), (0, 4)))
    rates = jnp.broadcast_to(rates[:, :, None], (L, 16, 128))

    vmem = pl.BlockSpec(memory_space=pltpu.VMEM)
    smem = pl.BlockSpec(memory_space=pltpu.SMEM)
    f32 = jnp.float32
    out, sums = pl.pallas_call(
        functools.partial(kernel, ny),
        out_shape=(
            jax.ShapeDtypeStruct((ROWS, 128), f32),
            jax.ShapeDtypeStruct((STEPS, 8, 128), f32),
        ),
        in_specs=[vmem] * 6 + [smem] * 2,
        out_specs=(vmem, vmem),
        scratch_shapes=[
            pltpu.VMEM((ROWS, 128), f32),
            pltpu.VMEM((ROWS, 128), f32),
            pltpu.VMEM((ROWS, 128), f32),
            pltpu.VMEM((4, 2 * L, 128), f32),
            pltpu.VMEM((L * 16, 128), f32),
            pltpu.VMEM((F, 2 * L, 128), jnp.bfloat16),
            pltpu.VMEM((L, 16, 128), f32),
            pltpu.VMEM((L, 16, 128), f32),
            pltpu.VMEM((STEPS, 4, SLAB, 128), f32),
            pltpu.VMEM((STEPS, 4, SLAB, 128), f32),
            pltpu.VMEM((NZ, SLAB, 128), f32),
            pltpu.VMEM((NZ, SLAB, 128), f32),
            pltpu.VMEM((16, STEPS, F * chunk, 128), jnp.bfloat16),
            pltpu.VMEM((16 * 40, 128), f32),
            pltpu.VMEM((ROWS, 128), f32),
            pltpu.VMEM((STEPS, 8, 128), f32),
            pltpu.VMEM((STEPS, ny - 1, 8, 128), f32),
            pltpu.VMEM((STEPS, 8, 128), f32),
            pltpu.VMEM((STEPS, NZ - 1, 8, 128), f32),
            pltpu.SemaphoreType.DMA((STEPS, 4)),
            pltpu.SemaphoreType.DMA((STEPS, 4)),
            pltpu.SemaphoreType.DMA((NZ,)),
            pltpu.SemaphoreType.DMA((NZ,)),
            pltpu.SemaphoreType.DMA((STEPS, 15)),
            pltpu.SemaphoreType.DMA((STEPS, 16)),
            pltpu.SemaphoreType.DMA((STEPS, ny - 1)),
            pltpu.SemaphoreType.DMA((STEPS, ny - 1)),
            pltpu.SemaphoreType.DMA((STEPS, NZ - 1)),
            pltpu.SemaphoreType.DMA((STEPS, NZ - 1)),
        ],
        compiler_params=pltpu.CompilerParams(collective_id=0, has_side_effects=True),
    )(
        state,
        wind,
        jnp.broadcast_to(insol, (8, 128)),
        impulses,
        weights,
        rates,
        coupling,
        recombination[None],
    )
    sums = sums[:, :, : ROWS // 8].transpose(0, 2, 1) / (tiles * 128)
    return out.reshape(1, F, L, 1, 128), sums.reshape(1, STEPS, F, L)


def solution(mesh):
    return jax.shard_map(
        per_device,
        mesh=mesh,
        in_specs=(
            P(None, None, "obj", "tile", None),
            P(None, None, "tile", None),
            P("tile", None),
            P("obj", "tile", None),
            P("obj"),
            P(),
            P(),
            P(),
            P(),
        ),
        out_specs=(P("obj", None, None, "tile", None), P("obj", None, None, None)),
        check_vma=False,
    )
```

```python
import functools

import jax
import jax.numpy as jnp
from jax import lax
from jax.experimental import pallas as pl
from jax.experimental.pallas import tpu as pltpu
from jax.sharding import PartitionSpec as P

smoothing = 0.2
MESH = pl.DeviceIdType.MESH
F = 12
L = 48
ROWS = F * L
NZ = 8
LAT = 16
TILES = 9
SLAB = 72
STEPS = 6
CHUNK = 36
PRE = 56


def kernel(
    ny, cp_ref, wind_ref, insol_ref, mask_ref, arrive_ref, snr_ref, kb_ref, coup_ref, rec_ref,
    out_ref, grad_ref,
    adj, adv, sol, coef, inv, mats, fwd, piv, edge_out, edge_in, swap_out, swap_in,
    pre, pre_out, pre_in, post, gathered, loose, state, sum_out, sum_y, part_out, sum_z,
    send_sem, recv_sem, swap_send, swap_recv, gather_send, gather_recv,
    y_send, y_recv, z_send, z_recv, pre_send, pre_recv,
):
    obj = lax.axis_index("obj")
    tile = lax.axis_index("tile")
    y = tile // NZ
    z = lax.rem(tile, NZ)
    east = lax.rem(y + 1, ny) * NZ + z
    west = lax.rem(y + ny - 1, ny) * NZ + z
    x = obj // 4
    far = lax.rem(obj // 2, 2)
    core = lax.rem(obj, 2)

    def chunk(at_x, at_far, at_core):
        return at_x * 4 + at_far * 2 + at_core

    partner = chunk(x, 1 - far, core)
    other = chunk(x, far, 1 - core)
    beside = [chunk(lax.rem(x + h, 4), far, core) for h in range(1, 4)]

    edge_in[...] = jnp.zeros_like(edge_in)
    barrier = pltpu.get_barrier_semaphore()
    for peer in [partner, other] + beside:
        pl.semaphore_signal(barrier, inc=1, device_id=(peer, tile), device_id_type=MESH)
    for hop in range(1, ny):
        peer = lax.rem(y + hop, ny) * NZ + z
        pl.semaphore_signal(barrier, inc=1, device_id=(obj, peer), device_id_type=MESH)
    for hop in range(1, NZ):
        peer = y * NZ + lax.rem(z + hop, NZ)
        pl.semaphore_signal(barrier, inc=1, device_id=(obj, peer), device_id_type=MESH)

    lane = lax.broadcasted_iota(jnp.int32, (8, 128), 1)
    block = lane // LAT
    inside = lax.rem(lane, LAT)

    def at(k, j, slab=SLAB):
        return pl.ds(pl.multiple_of(slab * k + 8 * j, 8), 8)

    def spread(source, slab, target):
        def body(j, c):
            rolled = [source[at(k, j, slab), :] for k in range(8)]
            rolled = [pltpu.roll(v, 16 * k, 1) if k else v for k, v in enumerate(rolled)]
            for d in range(NZ):
                piece = rolled[0]
                for k in range(1, 8):
                    piece = jnp.where(block == (d + k) % 8, rolled[k], piece)
                target[d, pl.ds(pl.multiple_of(8 * j, 8), 8), :] = piece
            return c

        lax.fori_loop(0, slab // 8, body, 0)

    def swap_copy(source, target, sent, got, hop):
        peer = lax.rem(z + hop, NZ)
        return pltpu.make_async_remote_copy(
            src_ref=source.at[peer],
            dst_ref=target.at[hop],
            send_sem=sent.at[hop],
            recv_sem=got.at[hop],
            device_id=(obj, y * NZ + peer),
            device_id_type=MESH,
        )

    def collect(source, slab, target):
        def body(j, c):
            got = [
                pltpu.roll(
                    source[hop, pl.ds(pl.multiple_of(8 * j, 8), 8), :],
                    lax.rem(256 - 16 * (z + hop), 128),
                    1,
                )
                for hop in range(NZ)
            ]
            for k in range(8):
                held = got[0]
                for hop in range(1, NZ):
                    held = jnp.where(block == (k - hop) % 8, got[hop], held)
                target[at(k, j, slab), :] = pltpu.roll(
                    held, lax.rem(16 * z + 128 - 16 * k, 128), 1
                )
            return c

        lax.fori_loop(0, slab // 8, body, 0)

    pre[...] = jnp.zeros_like(pre)
    for s in range(STEPS):
        pre[pl.ds(PRE * s, CHUNK), :] = cp_ref[s].astype(jnp.float32)
    pre[pl.ds(6 * PRE, L), :] = wind_ref[0]
    pre[pl.ds(7 * PRE, L), :] = wind_ref[1]
    pre[pl.ds(6 * PRE + L, 1), :] = insol_ref[...]
    pre[pl.ds(7 * PRE + L, 1), :] = mask_ref[...].astype(jnp.float32)
    spread(pre, PRE, pre_out)
    pl.semaphore_wait(barrier, 5 + ny - 1 + NZ - 1)
    for hop in range(1, NZ):
        swap_copy(pre_out, pre_in, pre_send, pre_recv, hop).start()
    pre_in[0] = pre_out[z]

    unit = lax.broadcasted_iota(jnp.int32, (16, 128), 1)
    first = 1.0 / (1.0 + kb_ref[0])
    piv[0] = first
    fwd[0] = (unit == 0).astype(jnp.float32)

    def down(l, before):
        inverse, value = before
        below = kb_ref[l - 1]
        weight = below * inverse
        inverse = 1.0 / (1.0 + below + kb_ref[l] - below * weight)
        value = jnp.where(unit == l, 1.0, 0.0) + weight * value
        piv[l] = inverse
        fwd[l] = value
        return inverse, value

    last = lax.fori_loop(1, L, down, (first, (unit == 0).astype(jnp.float32)))
    bottom = last[1] * last[0]
    inv[pl.ds((L - 1) * 16, 16)] = bottom

    def up(i, after):
        l = L - 2 - i
        value = (fwd[l] + kb_ref[l] * after) * piv[l]
        inv[pl.ds(pl.multiple_of(l * 16, 16), 16)] = value
        return value

    lax.fori_loop(0, L - 1, up, bottom)
    for f in range(F):
        matrix = inv[pl.ds(f, L, stride=16), :]
        high = matrix.astype(jnp.bfloat16)
        mats[f, pl.ds(0, L)] = high
        mats[f, pl.ds(L, L)] = (matrix - high.astype(jnp.float32)).astype(jnp.bfloat16)

    adj[...] = jnp.zeros_like(adj)
    for hop in range(1, NZ):
        swap_copy(pre_out, pre_in, pre_send, pre_recv, hop).wait()
    collect(pre_in, PRE, post)
    for s in range(STEPS):
        gathered[obj, s] = post[pl.ds(PRE * s, CHUNK), :].astype(jnp.bfloat16)

    def gather_copy(s, n, slot, peer):
        return pltpu.make_async_remote_copy(
            src_ref=gathered.at[slot, s],
            dst_ref=gathered.at[slot, s],
            send_sem=gather_send.at[s, n],
            recv_sem=gather_recv.at[s, slot],
            device_id=(peer, tile),
            device_id_type=MESH,
        )

    def near_slots():
        return [chunk(lax.rem(x + h, 4), w, core) for h in range(1, 4) for w in range(2)]

    def gather_own(s):
        for n, peer in enumerate([partner] + beside + [other]):
            gather_copy(s, n, obj, peer).start()

    def gather_far(s):
        gather_copy(s, 0, partner, partner).wait_recv()
        for n, peer in enumerate(beside + [other]):
            gather_copy(s, 5 + n, partner, peer).start()

    def gather_near(s):
        for n, slot in enumerate(near_slots()):
            gather_copy(s, 9 + n, slot, other).wait_recv()
            gather_copy(s, 9 + n, slot, other).start()

    def gather_end(s):
        for at_x in range(4):
            for w in range(2):
                gather_copy(s, 0, chunk(at_x, w, 1 - core), other).wait_recv()
        for slot in range(16):
            loose[pl.ds(40 * slot, CHUNK), :] = gathered[slot, s].astype(jnp.float32)
        for f in range(F):
            for i in range(3):
                state[pl.ds(f * L + i, 16, stride=3), :] = loose[
                    pl.ds(3 * f + i, 16, stride=40), :
                ]

    def send_own(t, c):
        gather_own(STEPS - 1 - t)
        return c

    lax.fori_loop(0, STEPS, send_own, 0)
    eastward = post[pl.ds(6 * PRE, L), :]
    northward = post[pl.ds(7 * PRE, L), :]
    for half in range(2):
        rows = pl.ds(half * L, L)
        coef[0, rows] = smoothing + 0.5 * eastward
        coef[1, rows] = smoothing - 0.5 * eastward
        coef[2, rows] = smoothing + 0.5 * northward
        coef[3, rows] = smoothing - 0.5 * northward

    def y_copy(s, hop):
        return pltpu.make_async_remote_copy(
            src_ref=sum_out.at[s],
            dst_ref=sum_y.at[s, hop - 1],
            send_sem=y_send.at[s, hop - 1],
            recv_sem=y_recv.at[s, hop - 1],
            device_id=(obj, lax.rem(y + hop, ny) * NZ + z),
            device_id_type=MESH,
        )

    def z_copy(s, hop):
        return pltpu.make_async_remote_copy(
            src_ref=part_out.at[s],
            dst_ref=sum_z.at[s, hop - 1],
            send_sem=z_send.at[s, hop - 1],
            recv_sem=z_recv.at[s, hop - 1],
            device_id=(obj, y * NZ + lax.rem(z + hop, NZ)),
            device_id_type=MESH,
        )

    def sums_on(s):
        total = sum_out[s]
        for hop in range(1, ny):
            y_copy(s, hop).wait()
            total = total + sum_y[s, hop - 1]
        part_out[s] = total
        for hop in range(1, NZ):
            z_copy(s, hop).start()

    def share(way, k, j):
        return coef[way, pl.ds(pl.multiple_of((SLAB * k) % L + 8 * j, 8), 8), :]

    def edge_copy(t, way, peer):
        return pltpu.make_async_remote_copy(
            src_ref=edge_out.at[t, way],
            dst_ref=edge_in.at[t, way],
            send_sem=send_sem.at[t, way],
            recv_sem=recv_sem.at[t, way],
            device_id=(obj, peer),
            device_id_type=MESH,
        )

    insol = post[pl.ds(6 * PRE + L, 1), :]
    mask = post[pl.ds(7 * PRE + L, 1), :]

    def step(t, carry):
        s = STEPS - 1 - t
        impulse = jnp.broadcast_to(arrive_ref[pl.ds(s, 1), :] * mask, (8, 128))

        def pack(j, c):
            held = [jnp.zeros((8, 128), jnp.float32)] * 4
            for k in range(8):
                a = adj[at(k, j), :] + snr_ref[at(k, j), :] * impulse
                adj[at(k, j), :] = a
                shifts = (16 * k, 16 * (k + 1), k, k - 15)
                for way in range(4):
                    moved = share(way, k, j) * a
                    turn = shifts[way] % 128
                    if turn:
                        moved = pltpu.roll(moved, turn, 1)
                    spot = block == k if way < 2 else inside == k
                    held[way] = jnp.where(spot, moved, held[way])
            for way in range(4):
                edge_out[t, way, pl.ds(pl.multiple_of(8 * j, 8), 8), :] = held[way]
            return c

        lax.fori_loop(0, TILES, pack, 0)
        edge_copy(t, 0, west).start()
        edge_copy(t, 1, east).start()

        @pl.when(z > 0)
        def _():
            edge_copy(t, 2, tile - 1).start()

        @pl.when(z < NZ - 1)
        def _():
            edge_copy(t, 3, tile + 1).start()

        def interior(j, c):
            for k in range(8):
                a = adj[at(k, j), :]
                to_west = pltpu.roll(share(0, k, j) * a, 128 - LAT, 1)
                to_east = pltpu.roll(share(1, k, j) * a, LAT, 1)
                to_south = pltpu.roll(share(2, k, j) * a, 127, 1)
                to_north = pltpu.roll(share(3, k, j) * a, 1, 1)
                adv[at(k, j), :] = (
                    (1.0 - 4.0 * smoothing) * a
                    + jnp.where(block < 7, to_west, 0.0)
                    + jnp.where(block > 0, to_east, 0.0)
                    + jnp.where(inside < LAT - 1, to_south, 0.0)
                    + jnp.where(inside > 0, to_north, 0.0)
                )
            return c

        lax.fori_loop(0, TILES, interior, 0)

        @pl.when(t == 0)
        def _():
            gather_far(STEPS - 1)
            gather_far(STEPS - 2)

        @pl.when((t > 0) & (t < STEPS - 1))
        def _():
            gather_near(s - 1)

        @pl.when((t > 0) & (t < STEPS - 2))
        def _():
            gather_far(s - 2)

        edge_copy(t, 0, west).wait()
        edge_copy(t, 1, east).wait()

        @pl.when(z > 0)
        def _():
            edge_copy(t, 2, tile - 1).wait_send()
            edge_copy(t, 3, tile - 1).wait_recv()

        @pl.when(z < NZ - 1)
        def _():
            edge_copy(t, 3, tile + 1).wait_send()
            edge_copy(t, 2, tile + 1).wait_recv()

        def turned(value, amount):
            return pltpu.roll(value, amount % 128, 1) if amount % 128 else value

        def unpack(j, c):
            got = [edge_in[t, way, pl.ds(pl.multiple_of(8 * j, 8), 8), :] for way in range(4)]
            for k in range(8):
                along = jnp.where(
                    block == 7,
                    turned(got[0], 112 - 16 * k),
                    jnp.where(block == 0, turned(got[1], -16 * k), 0.0),
                )
                across = jnp.where(
                    inside == LAT - 1,
                    turned(got[2], 15 - k),
                    jnp.where(inside == 0, turned(got[3], -k), 0.0),
                )
                adv[at(k, j), :] = adv[at(k, j), :] + along + across
            return c

        lax.fori_loop(0, TILES, unpack, 0)

        @pl.when(t > 0)
        def _():
            sums_on(s + 1)

        sums = jnp.zeros((8, 128), jnp.float32)
        for f in range(F):
            rows = pl.ds(f * L, L)
            x = adv[rows, :]
            high = x.astype(jnp.bfloat16)
            low = (x - high.astype(jnp.float32)).astype(jnp.bfloat16)
            both = jnp.dot(
                mats[f][:, :L],
                jnp.concatenate([high, low], axis=1),
                preferred_element_type=jnp.float32,
            )
            solved = both[:L, :128] + (both[:L, 128:] + both[L:, :128])
            sol[rows, :] = solved
            total = jnp.sum(solved * insol, axis=1, keepdims=True)
            for q in range(L // 8):
                sums = jnp.where(lane == f * (L // 8) + q, total[8 * q : 8 * q + 8], sums)
        sum_out[s] = sums
        for hop in range(1, ny):
            y_copy(s, hop).start()

        @pl.when(t == 0)
        def _():
            gather_near(STEPS - 1)
            gather_near(STEPS - 2)
            gather_far(STEPS - 3)

        gather_end(s)

        def mix(i, c):
            def spot(g):
                return pl.ds(pl.multiple_of(g * L + 16 * i, 16), 16)

            parts = [sol[spot(f), :] for f in range(F)]
            for g in range(F):
                total = parts[g] - (2.0 * rec_ref[0, g]) * (state[spot(g), :] * parts[g])
                for f in range(F):
                    total = total + coup_ref[f, g] * parts[f]
                adj[spot(g), :] = total
            return c

        lax.fori_loop(0, L // 16, mix, 0)
        return carry

    lax.fori_loop(0, STEPS, step, 0)

    spread(adj, SLAB, swap_out)
    for hop in range(1, NZ):
        swap_copy(swap_out, swap_in, swap_send, swap_recv, hop).start()
    swap_in[0] = swap_out[z]
    sums_on(0)
    for hop in range(1, NZ):
        swap_copy(swap_out, swap_in, swap_send, swap_recv, hop).wait()
    collect(swap_in, SLAB, out_ref)

    def finish(s, c):
        total = part_out[s]
        for hop in range(1, NZ):
            z_copy(s, hop).wait()
            total = total + sum_z[s, hop - 1]
        grad_ref[s] = total
        for n in range(15):
            gather_copy(s, n, obj, other).wait_send()
        return c

    lax.fori_loop(0, STEPS, finish, 0)


def per_device(
    checkpoints,
    courant,
    insolation,
    region_mask,
    measure_step,
    snr_weight,
    diffusion_number,
    coupling,
    recombination,
):
    tiles = lax.axis_size("tile")
    ny = tiles // NZ
    moments = jnp.arange(1, 9, dtype=jnp.int32)
    arrive = (measure_step[0] == moments).astype(jnp.float32)
    arrive = jnp.broadcast_to(arrive[:, None], (8, 128))
    weights = jnp.broadcast_to(snr_weight.reshape(ROWS, 1), (ROWS, 128))
    rates = jnp.pad(diffusion_number.T, ((0, 1), (0, 4)))
    rates = jnp.broadcast_to(rates[:, :, None], (L, 16, 128))

    vmem = pl.BlockSpec(memory_space=pltpu.VMEM)
    smem = pl.BlockSpec(memory_space=pltpu.SMEM)
    f32 = jnp.float32
    out, sums = pl.pallas_call(
        functools.partial(kernel, ny),
        out_shape=(
            jax.ShapeDtypeStruct((ROWS, 128), f32),
            jax.ShapeDtypeStruct((STEPS, 8, 128), f32),
        ),
        in_specs=[vmem] * 7 + [smem] * 2,
        out_specs=(vmem, vmem),
        scratch_shapes=[
            pltpu.VMEM((ROWS, 128), f32),
            pltpu.VMEM((ROWS, 128), f32),
            pltpu.VMEM((ROWS, 128), f32),
            pltpu.VMEM((4, 2 * L, 128), f32),
            pltpu.VMEM((L * 16, 128), f32),
            pltpu.VMEM((F, 2 * L, 128), jnp.bfloat16),
            pltpu.VMEM((L, 16, 128), f32),
            pltpu.VMEM((L, 16, 128), f32),
            pltpu.VMEM((STEPS, 4, SLAB, 128), f32),
            pltpu.VMEM((STEPS, 4, SLAB, 128), f32),
            pltpu.VMEM((NZ, SLAB, 128), f32),
            pltpu.VMEM((NZ, SLAB, 128), f32),
            pltpu.VMEM((8 * PRE, 128), f32),
            pltpu.VMEM((NZ, PRE, 128), f32),
            pltpu.VMEM((NZ, PRE, 128), f32),
            pltpu.VMEM((8 * PRE, 128), f32),
            pltpu.VMEM((16, STEPS, CHUNK, 128), jnp.bfloat16),
            pltpu.VMEM((16 * 40, 128), f32),
            pltpu.VMEM((ROWS, 128), f32),
            pltpu.VMEM((STEPS, 8, 128), f32),
            pltpu.VMEM((STEPS, ny - 1, 8, 128), f32),
            pltpu.VMEM((STEPS, 8, 128), f32),
            pltpu.VMEM((STEPS, NZ - 1, 8, 128), f32),
            pltpu.SemaphoreType.DMA((STEPS, 4)),
            pltpu.SemaphoreType.DMA((STEPS, 4)),
            pltpu.SemaphoreType.DMA((NZ,)),
            pltpu.SemaphoreType.DMA((NZ,)),
            pltpu.SemaphoreType.DMA((STEPS, 15)),
            pltpu.SemaphoreType.DMA((STEPS, 16)),
            pltpu.SemaphoreType.DMA((STEPS, ny - 1)),
            pltpu.SemaphoreType.DMA((STEPS, ny - 1)),
            pltpu.SemaphoreType.DMA((STEPS, NZ - 1)),
            pltpu.SemaphoreType.DMA((STEPS, NZ - 1)),
            pltpu.SemaphoreType.DMA((NZ,)),
            pltpu.SemaphoreType.DMA((NZ,)),
        ],
        compiler_params=pltpu.CompilerParams(collective_id=0, has_side_effects=True),
    )(
        checkpoints.reshape(STEPS, CHUNK, 128),
        courant.reshape(2, L, 128),
        insolation,
        region_mask[0],
        arrive,
        weights,
        rates,
        coupling,
        recombination[None],
    )
    sums = sums[:, :, : ROWS // 8].transpose(0, 2, 1) / (tiles * 128)
    return out.reshape(1, F, L, 1, 128), sums.reshape(1, STEPS, F, L)


def solution(mesh):
    return jax.shard_map(
        per_device,
        mesh=mesh,
        in_specs=(
            P(None, None, "obj", "tile", None),
            P(None, None, "tile", None),
            P("tile", None),
            P("obj", "tile", None),
            P("obj"),
            P(),
            P(),
            P(),
            P(),
        ),
        out_specs=(P("obj", None, None, "tile", None), P("obj", None, None, None)),
        check_vma=False,
    )
```

```python
import functools

import jax
import jax.numpy as jnp
from jax import lax
from jax.experimental import pallas as pl
from jax.experimental.pallas import tpu as pltpu
from jax.sharding import PartitionSpec as P

smoothing = 0.2
MESH = pl.DeviceIdType.MESH
F = 12
L = 48
ROWS = F * L
NZ = 8
LAT = 16
TILES = 9
SLAB = 72
STEPS = 6
CHUNK = 36
PRE = 56


def kernel(
    ny, cp_ref, wind_ref, insol_ref, mask_ref, arrive_ref, snr_ref, kb_ref, coup_ref, rec_ref,
    out_ref, grad_ref,
    adj, adv, sol, coef, inv, mats, fwd, piv, edge_out, edge_in, swap_out, swap_in,
    pre, pre_out, pre_in, post, gathered, loose, state, sum_out, sum_y, part_out, sum_z,
    send_sem, recv_sem, swap_send, swap_recv, gather_send, gather_recv,
    y_send, y_recv, z_send, z_recv, pre_send, pre_recv,
):
    obj = lax.axis_index("obj")
    tile = lax.axis_index("tile")
    y = tile // NZ
    z = lax.rem(tile, NZ)
    east = lax.rem(y + 1, ny) * NZ + z
    west = lax.rem(y + ny - 1, ny) * NZ + z
    x = obj // 4
    far = lax.rem(obj // 2, 2)
    core = lax.rem(obj, 2)

    def chunk(at_x, at_far, at_core):
        return at_x * 4 + at_far * 2 + at_core

    partner = chunk(x, 1 - far, core)
    other = chunk(x, far, 1 - core)
    beside = [chunk(lax.rem(x + h, 4), far, core) for h in range(1, 4)]

    edge_in[...] = jnp.zeros_like(edge_in)
    barrier = pltpu.get_barrier_semaphore()
    for peer in [partner, other] + beside:
        pl.semaphore_signal(barrier, inc=1, device_id=(peer, tile), device_id_type=MESH)
    for hop in range(1, ny):
        peer = lax.rem(y + hop, ny) * NZ + z
        pl.semaphore_signal(barrier, inc=1, device_id=(obj, peer), device_id_type=MESH)
    for hop in range(1, NZ):
        peer = y * NZ + lax.rem(z + hop, NZ)
        pl.semaphore_signal(barrier, inc=1, device_id=(obj, peer), device_id_type=MESH)

    lane = lax.broadcasted_iota(jnp.int32, (8, 128), 1)
    block = lane // LAT
    inside = lax.rem(lane, LAT)

    def at(k, j, slab=SLAB):
        return pl.ds(pl.multiple_of(slab * k + 8 * j, 8), 8)

    def spread(source, slab, target):
        def body(j, c):
            rolled = [source[at(k, j, slab), :] for k in range(8)]
            rolled = [pltpu.roll(v, 16 * k, 1) if k else v for k, v in enumerate(rolled)]
            for d in range(NZ):
                piece = rolled[0]
                for k in range(1, 8):
                    piece = jnp.where(block == (d + k) % 8, rolled[k], piece)
                target[d, pl.ds(pl.multiple_of(8 * j, 8), 8), :] = piece
            return c

        lax.fori_loop(0, slab // 8, body, 0)

    def swap_copy(source, target, sent, got, hop):
        peer = lax.rem(z + hop, NZ)
        return pltpu.make_async_remote_copy(
            src_ref=source.at[peer],
            dst_ref=target.at[hop],
            send_sem=sent.at[hop],
            recv_sem=got.at[hop],
            device_id=(obj, y * NZ + peer),
            device_id_type=MESH,
        )

    def collect(source, slab, target):
        def body(j, c):
            got = [
                pltpu.roll(
                    source[hop, pl.ds(pl.multiple_of(8 * j, 8), 8), :],
                    lax.rem(256 - 16 * (z + hop), 128),
                    1,
                )
                for hop in range(NZ)
            ]
            for k in range(8):
                held = got[0]
                for hop in range(1, NZ):
                    held = jnp.where(block == (k - hop) % 8, got[hop], held)
                target[at(k, j, slab), :] = pltpu.roll(
                    held, lax.rem(16 * z + 128 - 16 * k, 128), 1
                )
            return c

        lax.fori_loop(0, slab // 8, body, 0)

    pre[...] = jnp.zeros_like(pre)
    for s in range(STEPS):
        pre[pl.ds(PRE * s, CHUNK), :] = cp_ref[s].astype(jnp.float32)
    pre[pl.ds(6 * PRE, L), :] = wind_ref[0]
    pre[pl.ds(7 * PRE, L), :] = wind_ref[1]
    pre[pl.ds(6 * PRE + L, 1), :] = insol_ref[...]
    pre[pl.ds(7 * PRE + L, 1), :] = mask_ref[...].astype(jnp.float32)
    spread(pre, PRE, pre_out)
    pl.semaphore_wait(barrier, 5 + ny - 1 + NZ - 1)
    for hop in range(1, NZ):
        swap_copy(pre_out, pre_in, pre_send, pre_recv, hop).start()
    pre_in[0] = pre_out[z]

    unit = lax.broadcasted_iota(jnp.int32, (16, 128), 1)
    first = 1.0 / (1.0 + kb_ref[0])
    piv[0] = first
    fwd[0] = (unit == 0).astype(jnp.float32)

    def down(l, before):
        inverse, value = before
        below = kb_ref[l - 1]
        weight = below * inverse
        inverse = 1.0 / (1.0 + below + kb_ref[l] - below * weight)
        value = jnp.where(unit == l, 1.0, 0.0) + weight * value
        piv[l] = inverse
        fwd[l] = value
        return inverse, value

    last = lax.fori_loop(1, L, down, (first, (unit == 0).astype(jnp.float32)))
    bottom = last[1] * last[0]
    inv[pl.ds((L - 1) * 16, 16)] = bottom

    def up(i, after):
        l = L - 2 - i
        value = (fwd[l] + kb_ref[l] * after) * piv[l]
        inv[pl.ds(pl.multiple_of(l * 16, 16), 16)] = value
        return value

    lax.fori_loop(0, L - 1, up, bottom)
    for f in range(F):
        matrix = inv[pl.ds(f, L, stride=16), :]
        high = matrix.astype(jnp.bfloat16)
        mats[f, pl.ds(0, L)] = high
        mats[f, pl.ds(L, L)] = (matrix - high.astype(jnp.float32)).astype(jnp.bfloat16)

    adj[...] = jnp.zeros_like(adj)
    for hop in range(1, NZ):
        swap_copy(pre_out, pre_in, pre_send, pre_recv, hop).wait()
    collect(pre_in, PRE, post)
    for s in range(STEPS):
        gathered[obj, s] = post[pl.ds(PRE * s, CHUNK), :].astype(jnp.bfloat16)

    def gather_copy(s, n, slot, peer):
        return pltpu.make_async_remote_copy(
            src_ref=gathered.at[slot, s],
            dst_ref=gathered.at[slot, s],
            send_sem=gather_send.at[s, n],
            recv_sem=gather_recv.at[s, slot],
            device_id=(peer, tile),
            device_id_type=MESH,
        )

    def near_slots():
        return [chunk(lax.rem(x + h, 4), w, core) for h in range(1, 4) for w in range(2)]

    def gather_own(s):
        for n, peer in enumerate([partner] + beside + [other]):
            gather_copy(s, n, obj, peer).start()

    def gather_far(s):
        gather_copy(s, 0, partner, partner).wait_recv()
        for n, peer in enumerate(beside + [other]):
            gather_copy(s, 5 + n, partner, peer).start()

    def gather_near(s):
        for n, slot in enumerate(near_slots()):
            gather_copy(s, 9 + n, slot, other).wait_recv()
            gather_copy(s, 9 + n, slot, other).start()

    def gather_end(s):
        for at_x in range(4):
            for w in range(2):
                gather_copy(s, 0, chunk(at_x, w, 1 - core), other).wait_recv()
        for slot in range(16):
            loose[pl.ds(40 * slot, CHUNK), :] = gathered[slot, s].astype(jnp.float32)
        for f in range(F):
            for i in range(3):
                state[pl.ds(f * L + i, 16, stride=3), :] = loose[
                    pl.ds(3 * f + i, 16, stride=40), :
                ]

    def send_own(t, c):
        gather_own(STEPS - 1 - t)
        return c

    lax.fori_loop(0, STEPS, send_own, 0)
    eastward = post[pl.ds(6 * PRE, L), :]
    northward = post[pl.ds(7 * PRE, L), :]
    for half in range(2):
        rows = pl.ds(half * L, L)
        coef[0, rows] = smoothing + 0.5 * eastward
        coef[1, rows] = smoothing - 0.5 * eastward
        coef[2, rows] = smoothing + 0.5 * northward
        coef[3, rows] = smoothing - 0.5 * northward

    def y_copy(s, hop):
        return pltpu.make_async_remote_copy(
            src_ref=sum_out.at[s],
            dst_ref=sum_y.at[s, hop - 1],
            send_sem=y_send.at[s, hop - 1],
            recv_sem=y_recv.at[s, hop - 1],
            device_id=(obj, lax.rem(y + hop, ny) * NZ + z),
            device_id_type=MESH,
        )

    def z_copy(s, hop):
        return pltpu.make_async_remote_copy(
            src_ref=part_out.at[s],
            dst_ref=sum_z.at[s, hop - 1],
            send_sem=z_send.at[s, hop - 1],
            recv_sem=z_recv.at[s, hop - 1],
            device_id=(obj, y * NZ + lax.rem(z + hop, NZ)),
            device_id_type=MESH,
        )

    def sums_on(s):
        total = sum_out[s]
        for hop in range(1, ny):
            y_copy(s, hop).wait()
            total = total + sum_y[s, hop - 1]
        part_out[s] = total
        for hop in range(1, NZ):
            z_copy(s, hop).start()

    def share(way, k, j):
        return coef[way, pl.ds(pl.multiple_of((SLAB * k) % L + 8 * j, 8), 8), :]

    def edge_copy(t, way, peer):
        return pltpu.make_async_remote_copy(
            src_ref=edge_out.at[t, way],
            dst_ref=edge_in.at[t, way],
            send_sem=send_sem.at[t, way],
            recv_sem=recv_sem.at[t, way],
            device_id=(obj, peer),
            device_id_type=MESH,
        )

    insol = post[pl.ds(6 * PRE + L, 1), :]
    mask = post[pl.ds(7 * PRE + L, 1), :]

    def sums_of(s):
        sums = jnp.zeros((8, 128), jnp.float32)
        for f in range(F):
            total = jnp.sum(sol[pl.ds(f * L, L), :] * insol, axis=1, keepdims=True)
            for q in range(L // 8):
                sums = jnp.where(lane == f * (L // 8) + q, total[8 * q : 8 * q + 8], sums)
        sum_out[s] = sums
        for hop in range(1, ny):
            y_copy(s, hop).start()

    def step(t, carry):
        s = STEPS - 1 - t
        impulse = jnp.broadcast_to(arrive_ref[pl.ds(s, 1), :] * mask, (8, 128))

        def pack(j, c):
            held = [jnp.zeros((8, 128), jnp.float32)] * 4
            for k in range(8):
                a = adj[at(k, j), :] + snr_ref[at(k, j), :] * impulse
                adj[at(k, j), :] = a
                shifts = (16 * k, 16 * (k + 1), k, k - 15)
                for way in range(4):
                    moved = share(way, k, j) * a
                    turn = shifts[way] % 128
                    if turn:
                        moved = pltpu.roll(moved, turn, 1)
                    spot = block == k if way < 2 else inside == k
                    held[way] = jnp.where(spot, moved, held[way])
            for way in range(4):
                edge_out[t, way, pl.ds(pl.multiple_of(8 * j, 8), 8), :] = held[way]
            return c

        lax.fori_loop(0, TILES, pack, 0, unroll=9)
        edge_copy(t, 0, west).start()
        edge_copy(t, 1, east).start()

        @pl.when(z > 0)
        def _():
            edge_copy(t, 2, tile - 1).start()

        @pl.when(z < NZ - 1)
        def _():
            edge_copy(t, 3, tile + 1).start()

        def interior(j, c):
            for k in range(8):
                a = adj[at(k, j), :]
                to_west = pltpu.roll(share(0, k, j) * a, 128 - LAT, 1)
                to_east = pltpu.roll(share(1, k, j) * a, LAT, 1)
                to_south = pltpu.roll(share(2, k, j) * a, 127, 1)
                to_north = pltpu.roll(share(3, k, j) * a, 1, 1)
                adv[at(k, j), :] = (
                    (1.0 - 4.0 * smoothing) * a
                    + jnp.where(block < 7, to_west, 0.0)
                    + jnp.where(block > 0, to_east, 0.0)
                    + jnp.where(inside < LAT - 1, to_south, 0.0)
                    + jnp.where(inside > 0, to_north, 0.0)
                )
            return c

        lax.fori_loop(0, TILES, interior, 0, unroll=9)

        @pl.when(t == 0)
        def _():
            gather_far(STEPS - 1)
            gather_far(STEPS - 2)

        @pl.when((t > 0) & (t < STEPS - 1))
        def _():
            gather_near(s - 1)

        @pl.when((t > 0) & (t < STEPS - 2))
        def _():
            gather_far(s - 2)

        @pl.when(t > 0)
        def _():
            sums_of(s + 1)
            gather_end(s)

        @pl.when(t > 1)
        def _():
            sums_on(s + 2)

        edge_copy(t, 0, west).wait()
        edge_copy(t, 1, east).wait()

        @pl.when(z > 0)
        def _():
            edge_copy(t, 2, tile - 1).wait_send()
            edge_copy(t, 3, tile - 1).wait_recv()

        @pl.when(z < NZ - 1)
        def _():
            edge_copy(t, 3, tile + 1).wait_send()
            edge_copy(t, 2, tile + 1).wait_recv()

        def turned(value, amount):
            return pltpu.roll(value, amount % 128, 1) if amount % 128 else value

        def unpack(j, c):
            got = [edge_in[t, way, pl.ds(pl.multiple_of(8 * j, 8), 8), :] for way in range(4)]
            for k in range(8):
                along = jnp.where(
                    block == 7,
                    turned(got[0], 112 - 16 * k),
                    jnp.where(block == 0, turned(got[1], -16 * k), 0.0),
                )
                across = jnp.where(
                    inside == LAT - 1,
                    turned(got[2], 15 - k),
                    jnp.where(inside == 0, turned(got[3], -k), 0.0),
                )
                adv[at(k, j), :] = adv[at(k, j), :] + along + across
            return c

        lax.fori_loop(0, TILES, unpack, 0, unroll=9)

        for f in range(F):
            rows = pl.ds(f * L, L)
            x = adv[rows, :]
            high = x.astype(jnp.bfloat16)
            low = (x - high.astype(jnp.float32)).astype(jnp.bfloat16)
            both = jnp.dot(
                mats[f][:, :L],
                jnp.concatenate([high, low], axis=1),
                preferred_element_type=jnp.float32,
            )
            solved = both[:L, :128] + (both[:L, 128:] + both[L:, :128])
            sol[rows, :] = solved

        @pl.when(t == 0)
        def _():
            gather_near(STEPS - 1)
            gather_near(STEPS - 2)
            gather_far(STEPS - 3)
            gather_end(STEPS - 1)

        def mix(i, c):
            def spot(g):
                return pl.ds(pl.multiple_of(g * L + 16 * i, 16), 16)

            parts = [sol[spot(f), :] for f in range(F)]
            for g in range(F):
                total = parts[g] - (2.0 * rec_ref[0, g]) * (state[spot(g), :] * parts[g])
                for f in range(F):
                    total = total + coup_ref[f, g] * parts[f]
                adj[spot(g), :] = total
            return c

        lax.fori_loop(0, L // 16, mix, 0, unroll=True)
        return carry

    lax.fori_loop(0, STEPS, step, 0)

    spread(adj, SLAB, swap_out)
    for hop in range(1, NZ):
        swap_copy(swap_out, swap_in, swap_send, swap_recv, hop).start()
    sums_of(0)
    swap_in[0] = swap_out[z]
    sums_on(1)
    sums_on(0)
    for hop in range(1, NZ):
        swap_copy(swap_out, swap_in, swap_send, swap_recv, hop).wait()
    collect(swap_in, SLAB, out_ref)

    def finish(s, c):
        total = part_out[s]
        for hop in range(1, NZ):
            z_copy(s, hop).wait()
            total = total + sum_z[s, hop - 1]
        grad_ref[s] = total
        for n in range(15):
            gather_copy(s, n, obj, other).wait_send()
        return c

    lax.fori_loop(0, STEPS, finish, 0)


def per_device(
    checkpoints,
    courant,
    insolation,
    region_mask,
    measure_step,
    snr_weight,
    diffusion_number,
    coupling,
    recombination,
):
    tiles = lax.axis_size("tile")
    ny = tiles // NZ
    moments = jnp.arange(1, 9, dtype=jnp.int32)
    arrive = (measure_step[0] == moments).astype(jnp.float32)
    arrive = jnp.broadcast_to(arrive[:, None], (8, 128))
    weights = jnp.broadcast_to(snr_weight.reshape(ROWS, 1), (ROWS, 128))
    rates = jnp.pad(diffusion_number.T, ((0, 1), (0, 4)))
    rates = jnp.broadcast_to(rates[:, :, None], (L, 16, 128))

    vmem = pl.BlockSpec(memory_space=pltpu.VMEM)
    smem = pl.BlockSpec(memory_space=pltpu.SMEM)
    f32 = jnp.float32
    out, sums = pl.pallas_call(
        functools.partial(kernel, ny),
        out_shape=(
            jax.ShapeDtypeStruct((ROWS, 128), f32),
            jax.ShapeDtypeStruct((STEPS, 8, 128), f32),
        ),
        in_specs=[vmem] * 7 + [smem] * 2,
        out_specs=(vmem, vmem),
        scratch_shapes=[
            pltpu.VMEM((ROWS, 128), f32),
            pltpu.VMEM((ROWS, 128), f32),
            pltpu.VMEM((ROWS, 128), f32),
            pltpu.VMEM((4, 2 * L, 128), f32),
            pltpu.VMEM((L * 16, 128), f32),
            pltpu.VMEM((F, 2 * L, 128), jnp.bfloat16),
            pltpu.VMEM((L, 16, 128), f32),
            pltpu.VMEM((L, 16, 128), f32),
            pltpu.VMEM((STEPS, 4, SLAB, 128), f32),
            pltpu.VMEM((STEPS, 4, SLAB, 128), f32),
            pltpu.VMEM((NZ, SLAB, 128), f32),
            pltpu.VMEM((NZ, SLAB, 128), f32),
            pltpu.VMEM((8 * PRE, 128), f32),
            pltpu.VMEM((NZ, PRE, 128), f32),
            pltpu.VMEM((NZ, PRE, 128), f32),
            pltpu.VMEM((8 * PRE, 128), f32),
            pltpu.VMEM((16, STEPS, CHUNK, 128), jnp.bfloat16),
            pltpu.VMEM((16 * 40, 128), f32),
            pltpu.VMEM((ROWS, 128), f32),
            pltpu.VMEM((STEPS, 8, 128), f32),
            pltpu.VMEM((STEPS, ny - 1, 8, 128), f32),
            pltpu.VMEM((STEPS, 8, 128), f32),
            pltpu.VMEM((STEPS, NZ - 1, 8, 128), f32),
            pltpu.SemaphoreType.DMA((STEPS, 4)),
            pltpu.SemaphoreType.DMA((STEPS, 4)),
            pltpu.SemaphoreType.DMA((NZ,)),
            pltpu.SemaphoreType.DMA((NZ,)),
            pltpu.SemaphoreType.DMA((STEPS, 15)),
            pltpu.SemaphoreType.DMA((STEPS, 16)),
            pltpu.SemaphoreType.DMA((STEPS, ny - 1)),
            pltpu.SemaphoreType.DMA((STEPS, ny - 1)),
            pltpu.SemaphoreType.DMA((STEPS, NZ - 1)),
            pltpu.SemaphoreType.DMA((STEPS, NZ - 1)),
            pltpu.SemaphoreType.DMA((NZ,)),
            pltpu.SemaphoreType.DMA((NZ,)),
        ],
        compiler_params=pltpu.CompilerParams(collective_id=0, has_side_effects=True),
    )(
        checkpoints.reshape(STEPS, CHUNK, 128),
        courant.reshape(2, L, 128),
        insolation,
        region_mask[0],
        arrive,
        weights,
        rates,
        coupling,
        recombination[None],
    )
    sums = sums[:, :, : ROWS // 8].transpose(0, 2, 1) / (tiles * 128)
    return out.reshape(1, F, L, 1, 128), sums.reshape(1, STEPS, F, L)


def solution(mesh):
    return jax.shard_map(
        per_device,
        mesh=mesh,
        in_specs=(
            P(None, None, "obj", "tile", None),
            P(None, None, "tile", None),
            P("tile", None),
            P("obj", "tile", None),
            P("obj"),
            P(),
            P(),
            P(),
            P(),
        ),
        out_specs=(P("obj", None, None, "tile", None), P("obj", None, None, None)),
        check_vma=False,
    )
```

```python
import functools

import jax
import jax.numpy as jnp
from jax import lax
from jax.experimental import pallas as pl
from jax.experimental.pallas import tpu as pltpu
from jax.sharding import PartitionSpec as P

smoothing = 0.2
MESH = pl.DeviceIdType.MESH
F = 12
L = 48
ROWS = F * L
NZ = 8
LAT = 16
TILES = 9
SLAB = 72
STEPS = 6
CHUNK = 36
PRE = 40
PIECES = (
    (0, 0, 40, 6, 0), (0, 40, 4, 0, 36), (0, 44, 4, 1, 36),
    (1, 0, 40, 7, 0), (1, 40, 4, 2, 36), (1, 44, 4, 3, 36),
)
INSOL = 4 * PRE + 36
MASK = 4 * PRE + 37


def kernel(
    ny, cp_ref, wind_ref, insol_ref, mask_ref, arrive_ref, snr_ref, kb_ref, coup_ref, rec_ref,
    out_ref, grad_ref,
    adj, adv, sol, coef, inv, mats, fwd, piv, edge_out, edge_in, swap_out, swap_in,
    pre, pre_out, pre_in, post, gathered, loose, state, sum_out, sum_y, part_out, sum_z,
    send_sem, recv_sem, swap_send, swap_recv, gather_send, gather_recv,
    y_send, y_recv, z_send, z_recv, pre_send, pre_recv,
):
    obj = lax.axis_index("obj")
    tile = lax.axis_index("tile")
    y = tile // NZ
    z = lax.rem(tile, NZ)
    east = lax.rem(y + 1, ny) * NZ + z
    west = lax.rem(y + ny - 1, ny) * NZ + z
    x = obj // 4
    far = lax.rem(obj // 2, 2)
    core = lax.rem(obj, 2)

    def chunk(at_x, at_far, at_core):
        return at_x * 4 + at_far * 2 + at_core

    partner = chunk(x, 1 - far, core)
    other = chunk(x, far, 1 - core)
    beside = [chunk(lax.rem(x + h, 4), far, core) for h in range(1, 4)]

    edge_in[...] = jnp.zeros_like(edge_in)
    barrier = pltpu.get_barrier_semaphore()
    for peer in [partner, other] + beside:
        pl.semaphore_signal(barrier, inc=1, device_id=(peer, tile), device_id_type=MESH)
    for hop in range(1, ny):
        peer = lax.rem(y + hop, ny) * NZ + z
        pl.semaphore_signal(barrier, inc=1, device_id=(obj, peer), device_id_type=MESH)
    for hop in range(1, NZ):
        peer = y * NZ + lax.rem(z + hop, NZ)
        pl.semaphore_signal(barrier, inc=1, device_id=(obj, peer), device_id_type=MESH)

    lane = lax.broadcasted_iota(jnp.int32, (8, 128), 1)
    block = lane // LAT
    inside = lax.rem(lane, LAT)

    def at(k, j, slab=SLAB):
        return pl.ds(pl.multiple_of(slab * k + 8 * j, 8), 8)

    def spread(source, slab, target):
        def body(j, c):
            rolled = [source[at(k, j, slab), :] for k in range(8)]
            rolled = [pltpu.roll(v, 16 * k, 1) if k else v for k, v in enumerate(rolled)]
            for d in range(NZ):
                piece = rolled[0]
                for k in range(1, 8):
                    piece = jnp.where(block == (d + k) % 8, rolled[k], piece)
                target[d, pl.ds(pl.multiple_of(8 * j, 8), 8), :] = piece
            return c

        lax.fori_loop(0, slab // 8, body, 0)

    def swap_copy(source, target, sent, got, hop):
        peer = lax.rem(z + hop, NZ)
        return pltpu.make_async_remote_copy(
            src_ref=source.at[peer],
            dst_ref=target.at[hop],
            send_sem=sent.at[hop],
            recv_sem=got.at[hop],
            device_id=(obj, y * NZ + peer),
            device_id_type=MESH,
        )

    def collect(source, slab, target):
        def body(j, c):
            got = [
                pltpu.roll(
                    source[hop, pl.ds(pl.multiple_of(8 * j, 8), 8), :],
                    lax.rem(256 - 16 * (z + hop), 128),
                    1,
                )
                for hop in range(NZ)
            ]
            for k in range(8):
                held = got[0]
                for hop in range(1, NZ):
                    held = jnp.where(block == (k - hop) % 8, got[hop], held)
                target[at(k, j, slab), :] = pltpu.roll(
                    held, lax.rem(16 * z + 128 - 16 * k, 128), 1
                )
            return c

        lax.fori_loop(0, slab // 8, body, 0)

    pre[...] = jnp.zeros_like(pre)
    for s in range(STEPS):
        pre[pl.ds(PRE * s, CHUNK), :] = cp_ref[s].astype(jnp.float32)
    for part, level, count, slab, row in PIECES:
        pre[pl.ds(slab * PRE + row, count), :] = wind_ref[part, pl.ds(level, count), :]
    pre[pl.ds(INSOL, 1), :] = insol_ref[...]
    pre[pl.ds(MASK, 1), :] = mask_ref[...].astype(jnp.float32)
    spread(pre, PRE, pre_out)
    pl.semaphore_wait(barrier, 5 + ny - 1 + NZ - 1)
    for hop in range(1, NZ):
        swap_copy(pre_out, pre_in, pre_send, pre_recv, hop).start()
    pre_in[0] = pre_out[z]

    unit = lax.broadcasted_iota(jnp.int32, (16, 128), 1)
    first = 1.0 / (1.0 + kb_ref[0])
    piv[0] = first
    fwd[0] = (unit == 0).astype(jnp.float32)

    def down(l, before):
        inverse, value = before
        below = kb_ref[l - 1]
        weight = below * inverse
        inverse = 1.0 / (1.0 + below + kb_ref[l] - below * weight)
        value = jnp.where(unit == l, 1.0, 0.0) + weight * value
        piv[l] = inverse
        fwd[l] = value
        return inverse, value

    last = lax.fori_loop(1, L, down, (first, (unit == 0).astype(jnp.float32)))
    bottom = last[1] * last[0]
    inv[pl.ds((L - 1) * 16, 16)] = bottom

    def up(i, after):
        l = L - 2 - i
        value = (fwd[l] + kb_ref[l] * after) * piv[l]
        inv[pl.ds(pl.multiple_of(l * 16, 16), 16)] = value
        return value

    lax.fori_loop(0, L - 1, up, bottom)
    for f in range(F):
        matrix = inv[pl.ds(f, L, stride=16), :]
        high = matrix.astype(jnp.bfloat16)
        mats[f, pl.ds(0, L)] = high
        mats[f, pl.ds(L, L)] = (matrix - high.astype(jnp.float32)).astype(jnp.bfloat16)

    adj[...] = jnp.zeros_like(adj)
    for hop in range(1, NZ):
        swap_copy(pre_out, pre_in, pre_send, pre_recv, hop).wait()
    collect(pre_in, PRE, post)
    for s in range(STEPS):
        gathered[obj, s] = post[pl.ds(PRE * s, CHUNK), :].astype(jnp.bfloat16)

    def gather_copy(s, n, slot, peer):
        return pltpu.make_async_remote_copy(
            src_ref=gathered.at[slot, s],
            dst_ref=gathered.at[slot, s],
            send_sem=gather_send.at[s, n],
            recv_sem=gather_recv.at[s, slot],
            device_id=(peer, tile),
            device_id_type=MESH,
        )

    def near_slots():
        return [chunk(lax.rem(x + h, 4), w, core) for h in range(1, 4) for w in range(2)]

    def gather_own(s):
        for n, peer in enumerate([partner] + beside + [other]):
            gather_copy(s, n, obj, peer).start()

    def gather_far(s):
        gather_copy(s, 0, partner, partner).wait_recv()
        for n, peer in enumerate(beside + [other]):
            gather_copy(s, 5 + n, partner, peer).start()

    def gather_near(s):
        for n, slot in enumerate(near_slots()):
            gather_copy(s, 9 + n, slot, other).wait_recv()
            gather_copy(s, 9 + n, slot, other).start()

    def gather_end(s):
        for at_x in range(4):
            for w in range(2):
                gather_copy(s, 0, chunk(at_x, w, 1 - core), other).wait_recv()
        for slot in range(16):
            loose[pl.ds(40 * slot, CHUNK), :] = gathered[slot, s].astype(jnp.float32)
        for f in range(F):
            for i in range(3):
                state[pl.ds(f * L + i, 16, stride=3), :] = loose[
                    pl.ds(3 * f + i, 16, stride=40), :
                ]

    def send_own(t, c):
        gather_own(STEPS - 1 - t)
        return c

    lax.fori_loop(0, STEPS, send_own, 0)
    for part, level, count, slab, row in PIECES:
        wind = 0.5 * post[pl.ds(slab * PRE + row, count), :]
        for half in range(2):
            rows = pl.ds(half * L + level, count)
            coef[2 * part, rows, :] = smoothing + wind
            coef[2 * part + 1, rows, :] = smoothing - wind

    def y_copy(s, hop):
        return pltpu.make_async_remote_copy(
            src_ref=sum_out.at[s],
            dst_ref=sum_y.at[s, hop - 1],
            send_sem=y_send.at[s, hop - 1],
            recv_sem=y_recv.at[s, hop - 1],
            device_id=(obj, lax.rem(y + hop, ny) * NZ + z),
            device_id_type=MESH,
        )

    def z_copy(s, hop):
        return pltpu.make_async_remote_copy(
            src_ref=part_out.at[s],
            dst_ref=sum_z.at[s, hop - 1],
            send_sem=z_send.at[s, hop - 1],
            recv_sem=z_recv.at[s, hop - 1],
            device_id=(obj, y * NZ + lax.rem(z + hop, NZ)),
            device_id_type=MESH,
        )

    def sums_on(s):
        total = sum_out[s]
        for hop in range(1, ny):
            y_copy(s, hop).wait()
            total = total + sum_y[s, hop - 1]
        part_out[s] = total
        for hop in range(1, NZ):
            z_copy(s, hop).start()

    def share(way, k, j):
        return coef[way, pl.ds(pl.multiple_of((SLAB * k) % L + 8 * j, 8), 8), :]

    def edge_copy(t, way, peer):
        return pltpu.make_async_remote_copy(
            src_ref=edge_out.at[t, way],
            dst_ref=edge_in.at[t, way],
            send_sem=send_sem.at[t, way],
            recv_sem=recv_sem.at[t, way],
            device_id=(obj, peer),
            device_id_type=MESH,
        )

    insol = post[pl.ds(INSOL, 1), :]
    mask = post[pl.ds(MASK, 1), :]

    def sums_of(s):
        sums = jnp.zeros((8, 128), jnp.float32)
        for f in range(F):
            total = jnp.sum(sol[pl.ds(f * L, L), :] * insol, axis=1, keepdims=True)
            for q in range(L // 8):
                sums = jnp.where(lane == f * (L // 8) + q, total[8 * q : 8 * q + 8], sums)
        sum_out[s] = sums
        for hop in range(1, ny):
            y_copy(s, hop).start()

    def step(t, carry):
        s = STEPS - 1 - t
        impulse = jnp.broadcast_to(arrive_ref[pl.ds(s, 1), :] * mask, (8, 128))

        def pack(j, c):
            held = [jnp.zeros((8, 128), jnp.float32)] * 4
            for k in range(8):
                a = adj[at(k, j), :] + snr_ref[at(k, j), :] * impulse
                adj[at(k, j), :] = a
                shifts = (16 * k, 16 * (k + 1), k, k - 15)
                for way in range(4):
                    moved = share(way, k, j) * a
                    turn = shifts[way] % 128
                    if turn:
                        moved = pltpu.roll(moved, turn, 1)
                    spot = block == k if way < 2 else inside == k
                    held[way] = jnp.where(spot, moved, held[way])
            for way in range(4):
                edge_out[t, way, pl.ds(pl.multiple_of(8 * j, 8), 8), :] = held[way]
            return c

        lax.fori_loop(0, TILES, pack, 0, unroll=9)
        edge_copy(t, 0, west).start()
        edge_copy(t, 1, east).start()

        @pl.when(z > 0)
        def _():
            edge_copy(t, 2, tile - 1).start()

        @pl.when(z < NZ - 1)
        def _():
            edge_copy(t, 3, tile + 1).start()

        def interior(j, c):
            for k in range(8):
                a = adj[at(k, j), :]
                to_west = pltpu.roll(share(0, k, j) * a, 128 - LAT, 1)
                to_east = pltpu.roll(share(1, k, j) * a, LAT, 1)
                to_south = pltpu.roll(share(2, k, j) * a, 127, 1)
                to_north = pltpu.roll(share(3, k, j) * a, 1, 1)
                adv[at(k, j), :] = (
                    (1.0 - 4.0 * smoothing) * a
                    + jnp.where(block < 7, to_west, 0.0)
                    + jnp.where(block > 0, to_east, 0.0)
                    + jnp.where(inside < LAT - 1, to_south, 0.0)
                    + jnp.where(inside > 0, to_north, 0.0)
                )
            return c

        lax.fori_loop(0, TILES, interior, 0, unroll=9)

        @pl.when(t == 0)
        def _():
            gather_far(STEPS - 1)
            gather_far(STEPS - 2)

        @pl.when((t > 0) & (t < STEPS - 1))
        def _():
            gather_near(s - 1)

        @pl.when((t > 0) & (t < STEPS - 2))
        def _():
            gather_far(s - 2)

        @pl.when(t > 0)
        def _():
            sums_of(s + 1)
            gather_end(s)

        @pl.when(t > 1)
        def _():
            sums_on(s + 2)

        edge_copy(t, 0, west).wait()
        edge_copy(t, 1, east).wait()

        @pl.when(z > 0)
        def _():
            edge_copy(t, 2, tile - 1).wait_send()
            edge_copy(t, 3, tile - 1).wait_recv()

        @pl.when(z < NZ - 1)
        def _():
            edge_copy(t, 3, tile + 1).wait_send()
            edge_copy(t, 2, tile + 1).wait_recv()

        def turned(value, amount):
            return pltpu.roll(value, amount % 128, 1) if amount % 128 else value

        def unpack(j, c):
            got = [edge_in[t, way, pl.ds(pl.multiple_of(8 * j, 8), 8), :] for way in range(4)]
            for k in range(8):
                along = jnp.where(
                    block == 7,
                    turned(got[0], 112 - 16 * k),
                    jnp.where(block == 0, turned(got[1], -16 * k), 0.0),
                )
                across = jnp.where(
                    inside == LAT - 1,
                    turned(got[2], 15 - k),
                    jnp.where(inside == 0, turned(got[3], -k), 0.0),
                )
                adv[at(k, j), :] = adv[at(k, j), :] + along + across
            return c

        lax.fori_loop(0, TILES, unpack, 0, unroll=9)

        for f in range(F):
            rows = pl.ds(f * L, L)
            x = adv[rows, :]
            high = x.astype(jnp.bfloat16)
            low = (x - high.astype(jnp.float32)).astype(jnp.bfloat16)
            both = jnp.dot(
                mats[f][:, :L],
                jnp.concatenate([high, low], axis=1),
                preferred_element_type=jnp.float32,
            )
            solved = both[:L, :128] + (both[:L, 128:] + both[L:, :128])
            sol[rows, :] = solved

        @pl.when(t == 0)
        def _():
            gather_near(STEPS - 1)
            gather_near(STEPS - 2)
            gather_far(STEPS - 3)
            gather_end(STEPS - 1)

        def mix(i, c):
            def spot(g):
                return pl.ds(pl.multiple_of(g * L + 16 * i, 16), 16)

            parts = [sol[spot(f), :] for f in range(F)]
            for g in range(F):
                total = parts[g] - (2.0 * rec_ref[0, g]) * (state[spot(g), :] * parts[g])
                for f in range(F):
                    total = total + coup_ref[f, g] * parts[f]
                adj[spot(g), :] = total
            return c

        lax.fori_loop(0, L // 16, mix, 0, unroll=True)
        return carry

    lax.fori_loop(0, STEPS, step, 0)

    spread(adj, SLAB, swap_out)
    for hop in range(1, NZ):
        swap_copy(swap_out, swap_in, swap_send, swap_recv, hop).start()
    sums_of(0)
    swap_in[0] = swap_out[z]
    sums_on(1)
    sums_on(0)
    for hop in range(1, NZ):
        swap_copy(swap_out, swap_in, swap_send, swap_recv, hop).wait()
    collect(swap_in, SLAB, out_ref)

    def finish(s, c):
        total = part_out[s]
        for hop in range(1, NZ):
            z_copy(s, hop).wait()
            total = total + sum_z[s, hop - 1]
        grad_ref[s] = total
        for n in range(15):
            gather_copy(s, n, obj, other).wait_send()
        return c

    lax.fori_loop(0, STEPS, finish, 0)


def per_device(
    checkpoints,
    courant,
    insolation,
    region_mask,
    measure_step,
    snr_weight,
    diffusion_number,
    coupling,
    recombination,
):
    tiles = lax.axis_size("tile")
    ny = tiles // NZ
    moments = jnp.arange(1, 9, dtype=jnp.int32)
    arrive = (measure_step[0] == moments).astype(jnp.float32)
    arrive = jnp.broadcast_to(arrive[:, None], (8, 128))
    weights = jnp.broadcast_to(snr_weight.reshape(ROWS, 1), (ROWS, 128))
    rates = jnp.pad(diffusion_number.T, ((0, 1), (0, 4)))
    rates = jnp.broadcast_to(rates[:, :, None], (L, 16, 128))

    vmem = pl.BlockSpec(memory_space=pltpu.VMEM)
    smem = pl.BlockSpec(memory_space=pltpu.SMEM)
    f32 = jnp.float32
    out, sums = pl.pallas_call(
        functools.partial(kernel, ny),
        out_shape=(
            jax.ShapeDtypeStruct((ROWS, 128), f32),
            jax.ShapeDtypeStruct((STEPS, 8, 128), f32),
        ),
        in_specs=[vmem] * 7 + [smem] * 2,
        out_specs=(vmem, vmem),
        scratch_shapes=[
            pltpu.VMEM((ROWS, 128), f32),
            pltpu.VMEM((ROWS, 128), f32),
            pltpu.VMEM((ROWS, 128), f32),
            pltpu.VMEM((4, 2 * L, 128), f32),
            pltpu.VMEM((L * 16, 128), f32),
            pltpu.VMEM((F, 2 * L, 128), jnp.bfloat16),
            pltpu.VMEM((L, 16, 128), f32),
            pltpu.VMEM((L, 16, 128), f32),
            pltpu.VMEM((STEPS, 4, SLAB, 128), f32),
            pltpu.VMEM((STEPS, 4, SLAB, 128), f32),
            pltpu.VMEM((NZ, SLAB, 128), f32),
            pltpu.VMEM((NZ, SLAB, 128), f32),
            pltpu.VMEM((8 * PRE, 128), f32),
            pltpu.VMEM((NZ, PRE, 128), f32),
            pltpu.VMEM((NZ, PRE, 128), f32),
            pltpu.VMEM((8 * PRE, 128), f32),
            pltpu.VMEM((16, STEPS, CHUNK, 128), jnp.bfloat16),
            pltpu.VMEM((16 * 40, 128), f32),
            pltpu.VMEM((ROWS, 128), f32),
            pltpu.VMEM((STEPS, 8, 128), f32),
            pltpu.VMEM((STEPS, ny - 1, 8, 128), f32),
            pltpu.VMEM((STEPS, 8, 128), f32),
            pltpu.VMEM((STEPS, NZ - 1, 8, 128), f32),
            pltpu.SemaphoreType.DMA((STEPS, 4)),
            pltpu.SemaphoreType.DMA((STEPS, 4)),
            pltpu.SemaphoreType.DMA((NZ,)),
            pltpu.SemaphoreType.DMA((NZ,)),
            pltpu.SemaphoreType.DMA((STEPS, 15)),
            pltpu.SemaphoreType.DMA((STEPS, 16)),
            pltpu.SemaphoreType.DMA((STEPS, ny - 1)),
            pltpu.SemaphoreType.DMA((STEPS, ny - 1)),
            pltpu.SemaphoreType.DMA((STEPS, NZ - 1)),
            pltpu.SemaphoreType.DMA((STEPS, NZ - 1)),
            pltpu.SemaphoreType.DMA((NZ,)),
            pltpu.SemaphoreType.DMA((NZ,)),
        ],
        compiler_params=pltpu.CompilerParams(collective_id=0, has_side_effects=True),
    )(
        checkpoints.reshape(STEPS, CHUNK, 128),
        courant.reshape(2, L, 128),
        insolation,
        region_mask[0],
        arrive,
        weights,
        rates,
        coupling,
        recombination[None],
    )
    sums = sums[:, :, : ROWS // 8].transpose(0, 2, 1) / (tiles * 128)
    return out.reshape(1, F, L, 1, 128), sums.reshape(1, STEPS, F, L)


def solution(mesh):
    return jax.shard_map(
        per_device,
        mesh=mesh,
        in_specs=(
            P(None, None, "obj", "tile", None),
            P(None, None, "tile", None),
            P("tile", None),
            P("obj", "tile", None),
            P("obj"),
            P(),
            P(),
            P(),
            P(),
        ),
        out_specs=(P("obj", None, None, "tile", None), P("obj", None, None, None)),
        check_vma=False,
    )
```
